32 devices in a mesh: row: 8 (over y, x, core), col: 4 (over z).
Axes of the slice: x: 2, y: 2, z: 4, core: 2. Of those that a mesh axis runs over, the one named last changes fastest.
Arguments:
- inputs: bfloat16 [4096, 2048], P('row', 'col'), may hold values from -6 to 6
- segment_ids: int32 [4096], P('row'), may hold values from 0 to 15, as said below
- norm_gain: float32 [2048], P('col'), may hold values from 0.25 to 1.75
- query_weight: bfloat16 [2048, 2048], P('row', 'col'), may hold values from -0.125 to 0.125
- key_weight: bfloat16 [2048, 2048], P('row', 'col'), may hold values from -0.125 to 0.125
- value_weight: bfloat16 [2048, 4096], P('row', 'col'), may hold values from -0.125 to 0.125
- gate_weight: bfloat16 [2048, 4096], P('row', 'col'), may hold values from -0.125 to 0.125
- decay_weight: bfloat16 [2048, 16], P('row', 'col'), may hold values from -0.125 to 0.125
- beta_weight: bfloat16 [2048, 16], P('row', 'col'), may hold values from -0.125 to 0.125
- query_conv: float32 [4, 2048], P(None, 'col'), may hold values from -3 to 3
- key_conv: float32 [4, 2048], P(None, 'col'), may hold values from -3 to 3
- value_conv: float32 [4, 4096], P(None, 'col'), may hold values from -3 to 3
- decay_log: float32 [16], P('col'), may hold values from -4.5 to 0
- decay_bias: float32 [16], P('col'), may hold values from -6 to -1
- head_gain: float32 [256], replicated, may hold values from 0.25 to 1.75
- out_weight: bfloat16 [4096, 2048], P('col', 'row'), may hold values from -0.125 to 0.125
- second_gain: float32 [2048], P('col'), may hold values from 0.25 to 1.75
- hidden_gate: bfloat16 [2048, 5504], P('row', 'col'), may hold values from -0.125 to 0.125
- hidden_up: bfloat16 [2048, 5504], P('row', 'col'), may hold values from -0.125 to 0.125
- hidden_down: bfloat16 [5504, 2048], P('col', 'row'), may hold values from -0.15625 to 0.15625
- cotangent: bfloat16 [4096, 2048], P('row', 'col'), may hold values from -6 to 6
Outputs:
- result: float32 [4096, 2048], P('row', 'col')
- grad_inputs: float32 [4096, 2048], P('row', 'col')
- grad_norm_gain: float32 [2048], P('col')
- grad_query_weight: float32 [2048, 2048], P('row', 'col')
- grad_key_weight: float32 [2048, 2048], P('row', 'col')
- grad_value_weight: float32 [2048, 4096], P('row', 'col')
- grad_gate_weight: float32 [2048, 4096], P('row', 'col')
- grad_decay_weight: float32 [2048, 16], P('row', 'col')
- grad_beta_weight: float32 [2048, 16], P('row', 'col')
- grad_query_conv: float32 [4, 2048], P(None, 'col')
- grad_key_conv: float32 [4, 2048], P(None, 'col')
- grad_value_conv: float32 [4, 4096], P(None, 'col')
- grad_decay_log: float32 [16], P('col')
- grad_decay_bias: float32 [16], P('col')
- grad_head_gain: float32 [256], replicated
- grad_out_weight: float32 [4096, 2048], P('col', 'row')
- grad_second_gain: float32 [2048], P('col')
- grad_hidden_gate: float32 [2048, 5504], P('row', 'col')
- grad_hidden_up: float32 [2048, 5504], P('row', 'col')
- grad_hidden_down: float32 [5504, 2048], P('col', 'row')
The draws below stay inside these ranges and needn't reach their ends.
Inputs may be any that keep to these rules, and one draw needn't show every extreme that they name: `segment_ids`: never falling; the tokens i * 512 to (i + 1) * 512 - 1 hold exactly the two segments 2 i and 2 i + 1, in that order, each nonempty, the second of 256 tokens or more.
All inputs are finite; a program needn't handle non-finite values.
Results may differ from the reference program's by a relative error of at most 0.015.
Values may be sent and summed in bfloat16 or wider, within the bound.
No kernel may reach another device: no remote copies, remote signals or barrier semaphores. Data moves between devices by JAX's collectives and lax.ppermute only.
A program may use at most 192 MiB of HBM per device.

```python
import jax
import jax.numpy as jnp
from jax import lax

D = 2048
HEADS = 16
DV = 256
FF = 5504
CH = 64
TOK_DEV = 512
QW = 2048
VW = 4096
TOKENS = 4096
N_ROW = 8


def draw_segment_ids(key, part):
    cuts = jax.random.randint(key, (TOKENS // TOK_DEV,), TOK_DEV // 8, TOK_DEV // 2 + 1)
    places = jnp.arange(TOKENS, dtype=jnp.int32)
    owner = places // TOK_DEV
    inside = places % TOK_DEV
    later = (inside >= cuts[owner]).astype(jnp.int32)
    return (2 * owner + later).astype(jnp.int32)


def strengthened(values, key, source, target, parts, factor):
    owner, partner = [(jnp.arange(values.shape[dim]) // (values.shape[dim] // parts)).reshape([-1 if axis == dim else 1 for axis in range(values.ndim)]) for dim in (source, target)]
    chosen = jax.random.permutation(key, parts)[partner]
    strong = (owner == chosen) | (owner == (partner + parts // 2) % parts)
    return jnp.where(strong, factor * values, values)


def level_of(rng, shape, cuts, low, top_value):
    def one(axis_at, parts):
        heights = jax.random.uniform(jax.random.fold_in(jax.random.fold_in(rng, 6), axis_at), (parts,), jnp.float32, low / len(cuts), top_value / len(cuts))
        return jnp.repeat(jnp.exp(heights), shape[axis_at] // parts).reshape((-1,) + (1,) * (len(shape) - axis_at - 1))

    factor_of = one(*cuts[0])
    for cut in cuts[1:]:
        factor_of = factor_of * one(*cut)
    return factor_of


def centred(key, dims, deviation, bound, pieces=(), held_as=jnp.bfloat16):
    values = deviation * jax.random.normal(key, dims, jnp.float32)
    if pieces:
        values = values * level_of(key, dims, pieces, -0.22, 0.18)
    return jnp.clip(values, -bound, bound).astype(held_as)


def bell_draw_with(key, shape, spread, reach, shards, heavy, held_as=jnp.bfloat16):
    values = spread * jax.random.normal(key, shape, jnp.float32)
    if shards:
        values = values * level_of(key, shape, shards, -0.22, 0.18)
    return jnp.clip(strengthened(values, jax.random.fold_in(key, 3), *heavy), -reach, reach).astype(held_as)


def setup_inputs(seed: int = 0) -> dict:
    arg_keys = jax.random.split(jax.random.key(seed), 22)
    inputs = bell_draw_with(arg_keys[0], (TOKENS, D), 1.0, 6.0, ((0, 8), (1, 4)), (0, 1, 8, 2.0))
    segment_ids = draw_segment_ids(jax.random.fold_in(arg_keys[21], 71), 0)
    norm_gain = jnp.clip(1.0 + 0.15 * jax.random.normal(arg_keys[2], (D,), jnp.float32), 0.25, 1.75)
    query_weight = centred(arg_keys[3], (D, QW), D ** -0.5, 0.125, ((0, 8), (1, 4)))
    key_weight = centred(arg_keys[4], (D, QW), D ** -0.5, 0.125, ((0, 8), (1, 4)))
    value_weight = centred(arg_keys[5], (D, VW), D ** -0.5, 0.125, ((0, 8), (1, 4)))
    gate_weight = centred(arg_keys[6], (D, VW), D ** -0.5, 0.125, ((0, 8), (1, 4)))
    decay_weight = centred(arg_keys[7], (D, HEADS), D ** -0.5, 0.125, ((0, 8), (1, 4)))
    beta_weight = centred(arg_keys[8], (D, HEADS), D ** -0.5, 0.125, ((0, 8), (1, 4)))
    query_conv = centred(arg_keys[9], (4, QW), 4 ** -0.5, 3.0, ((1, 4),), jnp.float32)
    key_conv = centred(arg_keys[10], (4, QW), 4 ** -0.5, 3.0, ((1, 4),), jnp.float32)
    value_conv = centred(arg_keys[11], (4, VW), 4 ** -0.5, 3.0, ((1, 4),), jnp.float32)
    decay_log = jnp.clip(-4.5 + 4.5 * jax.random.uniform(arg_keys[12], (HEADS,), jnp.float32) ** level_of(arg_keys[12], (HEADS,), ((0, 4),), -0.2, 0.2), -4.5, 0.0)
    decay_bias = jnp.clip(-6.0 + 5.0 * jax.random.uniform(arg_keys[13], (HEADS,), jnp.float32) ** level_of(arg_keys[13], (HEADS,), ((0, 4),), -0.2, 0.2), -6.0, -1.0)
    head_gain = jnp.clip(1.0 + 0.15 * jax.random.normal(arg_keys[14], (DV,), jnp.float32), 0.25, 1.75)
    out_weight = centred(arg_keys[15], (VW, D), (VW // 2) ** -0.5, 0.125, ((0, 4), (1, 8)))
    second_gain = jnp.clip(1.0 + 0.15 * jax.random.normal(arg_keys[16], (D,), jnp.float32), 0.25, 1.75)
    hidden_gate = centred(arg_keys[17], (D, FF), D ** -0.5, 0.125, ((0, 8), (1, 4)))
    hidden_up = centred(arg_keys[18], (D, FF), D ** -0.5, 0.125, ((0, 8), (1, 4)))
    hidden_down = centred(arg_keys[19], (FF, D), (FF // 4) ** -0.5, 0.15625, ((0, 4), (1, 8)))
    cotangent = bell_draw_with(arg_keys[20], (TOKENS, D), 1.0, 6.0, ((0, 8), (1, 4)), (0, 1, 8, 2.0))
    return dict(inputs=inputs, segment_ids=segment_ids, norm_gain=norm_gain, query_weight=query_weight, key_weight=key_weight, value_weight=value_weight, gate_weight=gate_weight, decay_weight=decay_weight, beta_weight=beta_weight, query_conv=query_conv, key_conv=key_conv, value_conv=value_conv, decay_log=decay_log, decay_bias=decay_bias, head_gain=head_gain, out_weight=out_weight, second_gain=second_gain, hidden_gate=hidden_gate, hidden_up=hidden_up, hidden_down=hidden_down, cotangent=cotangent)


HIGH = lax.Precision.HIGHEST

@jax.custom_vjp
def low(v):
    return lax.optimization_barrier(v.astype(jnp.bfloat16)).astype(jnp.float32)

@jax.custom_vjp
def low_back(v):
    return v

def low_keep(v):
    return (low(v), None)

def low_pass(kept, grad):
    return (grad,)

def back_keep(v):
    return (v, None)

def back_low(kept, grad):
    return (low(grad),)
low.defvjp(low_keep, low_pass)
low_back.defvjp(back_keep, back_low)

def rms_inverse(values, epsilon):
    return lax.rsqrt(lax.optimization_barrier(jnp.mean(values * values, axis=-1, keepdims=True)) + epsilon)

def causal_conv(series, kernel, segment_ids):
    total = series * kernel[3]
    for shift in (1, 2, 3):
        moved = jnp.concatenate([jnp.zeros((shift, series.shape[1]), series.dtype), series[:-shift]], axis=0)
        prior = jnp.concatenate([jnp.full((shift,), -1, jnp.int32), segment_ids[:-shift]], axis=0)
        total = total + jnp.where((prior == segment_ids)[:, None], moved, 0.0) * kernel[3 - shift]
    return total

def delta_rule(queries, keys_in, values, log_decay, betas, segment_ids):
    tokens, heads, key_size = queries.shape
    value_size = values.shape[2]
    groups = tokens // CH

    def by_block(array):
        return jnp.transpose(array.reshape(groups, CH, heads, array.shape[2]), (2, 0, 1, 3))
    query_blocks = by_block(queries)
    key_blocks = by_block(keys_in)
    value_blocks = by_block(values)
    decay_blocks = jnp.transpose(log_decay.reshape(groups, CH, heads), (2, 0, 1))
    beta_blocks = jnp.transpose(betas.reshape(groups, CH, heads), (2, 0, 1))
    seg_blocks = segment_ids.reshape(groups, CH)
    running = jnp.cumsum(decay_blocks, axis=2)
    rows_index = lax.broadcasted_iota(jnp.int32, (CH, CH), 0)
    cols_index = lax.broadcasted_iota(jnp.int32, (CH, CH), 1)
    same_seg = seg_blocks[:, :, None] == seg_blocks[:, None, :]
    keep_incl = same_seg & (rows_index >= cols_index)
    keep_strict = same_seg & (rows_index > cols_index)
    spread_decay = running[..., :, None] - running[..., None, :]
    decay_matrix = jnp.where(keep_incl, jnp.exp(jnp.minimum(spread_decay, 0.0)), 0.0)
    before = jnp.concatenate([seg_blocks[:1, :1] - 1, seg_blocks[:-1, -1:]], axis=0)
    carried = jnp.where(seg_blocks == before, jnp.exp(running), 0.0)
    key_inner = jnp.einsum('hnid,hnjd->hnij', key_blocks, key_blocks, precision=HIGH)
    lower_part = jnp.where(keep_strict, beta_blocks[..., :, None] * decay_matrix * key_inner, 0.0)
    identity = jnp.eye(CH, dtype=jnp.float32)
    right_side = jnp.concatenate([beta_blocks[..., None] * value_blocks, (beta_blocks * carried)[..., None] * key_blocks], axis=3)
    solved = jax.scipy.linalg.solve_triangular(identity + lower_part, right_side, lower=True, unit_diagonal=True)
    fresh = solved[..., :value_size]
    mixing = solved[..., value_size:]
    query_key = jnp.einsum('hnid,hnjd->hnij', query_blocks, key_blocks, precision=HIGH) * decay_matrix
    tail = decay_matrix[..., CH - 1, :]
    tail_state = carried[..., CH - 1]

    def advance(state, item):
        fresh_now, mixing_now, query_now, key_now, score_now, carried_now, tail_now, tail_keep = item
        written = fresh_now - jnp.einsum('hld,hdv->hlv', mixing_now, state, precision=HIGH)
        output = carried_now[..., None] * jnp.einsum('hld,hdv->hlv', query_now, state, precision=HIGH)
        output = output + jnp.einsum('hij,hjv->hiv', score_now, written, precision=HIGH)
        state = tail_keep[:, None, None] * state + jnp.einsum('hld,hlv->hdv', key_now * tail_now[..., None], written, precision=HIGH)
        return (state, output)
    items = tuple((jnp.moveaxis(array, 1, 0) for array in (fresh, mixing, query_blocks, key_blocks, query_key, carried, tail, tail_state)))
    start_state = jnp.zeros((heads, key_size, value_size), jnp.float32)
    unused, outputs = lax.scan(advance, start_state, items)
    return jnp.transpose(outputs, (0, 2, 1, 3)).reshape(tokens, heads, value_size)

def mixer(query_pre, key_pre, value_pre, gate_pre, decay_pre, beta_pre, query_conv, key_conv, value_conv, decay_log, decay_bias, head_gain, segment_ids):
    tokens = query_pre.shape[0]
    heads = decay_pre.shape[1]
    key_size = query_pre.shape[1] // heads
    value_size = value_pre.shape[1] // heads
    query_act = jax.nn.silu(causal_conv(query_pre, query_conv, segment_ids)).reshape(tokens, heads, key_size)
    key_act = jax.nn.silu(causal_conv(key_pre, key_conv, segment_ids)).reshape(tokens, heads, key_size)
    value_act = jax.nn.silu(causal_conv(value_pre, value_conv, segment_ids)).reshape(tokens, heads, value_size)
    queries = query_act * lax.rsqrt(lax.optimization_barrier(jnp.sum(query_act * query_act, axis=-1, keepdims=True)) + 1e-06) / jnp.sqrt(key_size * 1.0)
    keys_in = key_act * lax.rsqrt(lax.optimization_barrier(jnp.sum(key_act * key_act, axis=-1, keepdims=True)) + 1e-06)
    log_decay = -jnp.exp(decay_log) * jax.nn.softplus(decay_pre + decay_bias)
    betas = jax.nn.sigmoid(beta_pre)
    heads_out = delta_rule(queries, keys_in, value_act, log_decay, betas, segment_ids)
    heads_normed = heads_out * rms_inverse(heads_out, 1e-05) * head_gain
    return heads_normed.reshape(tokens, heads * value_size) * jax.nn.silu(gate_pre)

def reference(inputs, segment_ids, norm_gain, query_weight, key_weight, value_weight, gate_weight, decay_weight, beta_weight, query_conv, key_conv, value_conv, decay_log, decay_bias, head_gain, out_weight, second_gain, hidden_gate, hidden_up, hidden_down, cotangent):
    checked = jax.checkpoint(mixer)

    def forward(inputs, norm_gain, query_weight, key_weight, value_weight, gate_weight, decay_weight, beta_weight, query_conv, key_conv, value_conv, decay_log, decay_bias, head_gain, out_weight, second_gain, hidden_gate, hidden_up, hidden_down):
        hidden = low(inputs * rms_inverse(inputs, 1e-05) * norm_gain)
        projected = tuple((low_back(jnp.dot(hidden, weight_matrix, precision=HIGH)) for weight_matrix in (query_weight, key_weight, value_weight, gate_weight, decay_weight, beta_weight)))
        blocked = tuple((array.reshape(N_ROW, TOK_DEV, array.shape[1]) for array in projected))
        seg_rows = segment_ids.reshape(N_ROW, TOK_DEV)

        def run_block(item):
            return checked(item[0], item[1], item[2], item[3], item[4], item[5], query_conv, key_conv, value_conv, decay_log, decay_bias, head_gain, item[6])
        mixed = lax.map(run_block, blocked + (seg_rows,))
        mixed = low(mixed.reshape(N_ROW * TOK_DEV, mixed.shape[2]))
        residual = inputs + low_back(jnp.dot(mixed, out_weight, precision=HIGH))
        second = low(residual * rms_inverse(residual, 1e-05) * second_gain)
        gate_value = low_back(jnp.dot(second, hidden_gate, precision=HIGH))
        up_value = low_back(jnp.dot(second, hidden_up, precision=HIGH))
        product = low(jax.nn.silu(gate_value) * up_value)
        return residual + low_back(jnp.dot(product, hidden_down, precision=HIGH))
    floats = tuple((array.astype(jnp.float32) for array in (inputs, norm_gain, query_weight, key_weight, value_weight, gate_weight, decay_weight, beta_weight, query_conv, key_conv, value_conv, decay_log, decay_bias, head_gain, out_weight, second_gain, hidden_gate, hidden_up, hidden_down)))
    result, pullback = jax.vjp(forward, *floats)
    grads = pullback(cotangent.astype(jnp.float32))
    return (result, grads[0], grads[1], grads[2], grads[3], grads[4], grads[5], grads[6], grads[7], grads[8], grads[9], grads[10], grads[11], grads[12], grads[13], grads[14], grads[15], grads[16], grads[17], grads[18])
```

```python
import functools
import jax
import jax.numpy as jnp
from jax import lax
from jax.experimental import pallas as pl
from jax.experimental.pallas import tpu as pltpu
from jax.sharding import PartitionSpec as P

BF = jnp.bfloat16
F32 = jnp.float32
BLOCK = 128
VMEM = 56 * 1024 * 1024


def dot(left, right, lc=1, rc=0):
    return lax.dot_general(left, right, (((lc,), (rc,)), ((), ())), preferred_element_type=F32)


def split(x):
    high = x.astype(BF)
    return high, (x - high.astype(F32)).astype(BF)


def dot3(left, right, lc=1, rc=0):
    return (
        dot(left[0], right[0], lc, rc) + dot(left[0], right[1], lc, rc) + dot(left[1], right[0], lc, rc)
    )


def dotx(left, right, lc=1, rc=0):
    first = right.astype(BF)
    rest = right - first.astype(F32)
    second = rest.astype(BF)
    third = (rest - second.astype(F32)).astype(BF)
    return dot(left, first, lc, rc) + dot(left, second, lc, rc) + dot(left, third, lc, rc)


def sigmoid(x):
    return 0.5 + 0.5 * jnp.tanh(0.5 * x)


def lane_pick(block, lane):
    index = lax.broadcasted_iota(jnp.int32, block.shape, 1)
    return jnp.sum(jnp.where(index == lane, block, 0.0), axis=1, keepdims=True)


def row_pick(block, row):
    index = lax.broadcasted_iota(jnp.int32, block.shape, 0)
    return jnp.sum(jnp.where(index == row, block, 0.0), axis=0, keepdims=True)


def softplus(x):
    return jnp.maximum(x, 0.0) + jnp.log1p(jnp.exp(-jnp.abs(x)))


def conv_act(x, taps, marks):
    total = x * taps[3:4]
    for shift in (1, 2, 3):
        total = total + (marks[:, shift - 1 : shift] * pltpu.roll(x, shift, 0)) * taps[3 - shift : 4 - shift]
    gate = sigmoid(total)
    return total, gate


def grids():
    rows = lax.broadcasted_iota(jnp.int32, (BLOCK, BLOCK), 0)
    cols = lax.broadcasted_iota(jnp.int32, (BLOCK, BLOCK), 1)
    return rows, cols


def decays(small, params, head, heads):
    rate = jnp.exp(params[0:1])
    log_decay = -rate * softplus(small + params[1:2])
    beta = sigmoid(lane_pick(small, heads + head))
    return log_decay, beta


def block_decay(log_decay, head, rows, cols, seg_col, seg_row, last_seg):
    lower = (rows >= cols).astype(BF)
    running = dotx(lower, log_decay)
    column = lane_pick(running, head)
    line = row_pick(running.T, head)
    same = (seg_col == seg_row) & (rows >= cols)
    decay = jnp.where(same, jnp.exp(jnp.minimum(column - line, 0.0)), 0.0)
    carried = None
    if last_seg is not None:
        carried = jnp.where(seg_col == last_seg, jnp.exp(column), 0.0)
    return decay, carried


def unit_inverse(lower, rows, cols):
    identity = (rows == cols).astype(F32)
    base = 16
    near = jnp.where((rows // base) == (cols // base), -lower, 0.0)
    power = split(near)
    total = identity + near
    width = 2
    while width < base:
        power = split(dot3(power, power))
        total = total + dot3(split(total), power)
        width *= 2
    while base < BLOCK:
        pair = (rows // (2 * base) == cols // (2 * base)) & (rows // base != cols // base)
        off = split(jnp.where(pair, lower, 0.0))
        parts = split(total)
        total = total - dot3(parts, split(dot3(off, parts)))
        base *= 2
    return total


def heads_inputs(pre, taps, marks, dk):
    total, gate = conv_act(pre[:, : taps.shape[1]], taps, marks)
    act = total * gate
    query_act, key_act, values = act[:, :dk], act[:, dk : 2 * dk], act[:, 2 * dk :]
    query_scale = lax.rsqrt(jnp.sum(query_act * query_act, axis=1, keepdims=True) + 1e-06)
    key_scale = lax.rsqrt(jnp.sum(key_act * key_act, axis=1, keepdims=True) + 1e-06)
    return total, gate, query_act, key_act, values, query_scale, key_scale


def forward_kernel(heads, dk, dv, pre_ref, small_ref, taps_ref, marks_ref, segs_ref, params_ref, gain_ref,
                   mixed_ref, out_ref, fresh_ref, mats_ref, states_ref):
    head = pl.program_id(0)
    marks = marks_ref[...]
    pre = pre_ref[...]
    tokens = pre.shape[0]
    _, _, query_act, key_act, values, query_scale, key_scale = heads_inputs(pre, taps_ref[...], marks, dk)
    queries = query_act * (query_scale * dk ** -0.5)
    keys = key_act * key_scale
    log_decay, beta = decays(small_ref[...], params_ref[...], head, heads)
    rows, cols = grids()
    state = None
    for index in range(tokens // BLOCK):
        at = slice(index * BLOCK, (index + 1) * BLOCK)
        seg_col, seg_row = marks[at, 6:7], segs_ref[0:1, at]
        last_seg = marks[index * BLOCK - 1 : index * BLOCK, 6:7] if index else None
        decay, carried = block_decay(log_decay[at], head, rows, cols, seg_col, seg_row, last_seg)
        key, query, value, strength = keys[at], queries[at], values[at], beta[at]
        key_parts, query_parts = split(key), split(query)
        inner = jnp.where(rows > cols, dot3(key_parts, key_parts, 1, 1) * decay, 0.0)
        score = dot3(query_parts, key_parts, 1, 1) * decay
        inverse = unit_inverse(strength * inner, rows, cols)
        if index:
            state_parts = split(state)
            seen = dot3(key_parts, state_parts)
            asked = dot3(query_parts, state_parts)
            source = strength * (value - carried * seen)
        else:
            source = strength * value
        fresh = dot3(split(inverse), split(source))
        fresh_parts = split(fresh)
        output = dot3(split(score), fresh_parts)
        if index:
            output = output + carried * asked
        if index + 1 < tokens // BLOCK:
            tail = lane_pick_row(decay)
            grown = dot3(split(key * tail), fresh_parts, 0, 0)
            state = grown if state is None else carried[BLOCK - 1 : BLOCK] * state + grown
            states_ref[index * dk : (index + 1) * dk, :] = state
        fresh_ref[at, :] = fresh
        mats_ref[at, 0:BLOCK] = inner
        mats_ref[at, BLOCK : 2 * BLOCK] = score
        mats_ref[at, 2 * BLOCK :] = inverse
        out_ref[at, :] = output
        scale = lax.rsqrt(jnp.mean(output * output, axis=1, keepdims=True) + 1e-05)
        gate_pre = pre[at, 2 * dk + dv :]
        mixed_ref[at, :] = (output * scale * gain_ref[0:1] * (gate_pre * sigmoid(gate_pre))).astype(BF)


def lane_pick_row(decay):
    return decay.T[:, BLOCK - 1 : BLOCK]


def backward_kernel(heads, dk, dv, pre_ref, small_ref, taps_ref, marks_ref, segs_ref, params_ref, gain_ref,
                    grad_ref, out_ref, fresh_ref, mats_ref, states_ref,
                    low_ref, low_small_ref, taps_grad_ref, params_grad_ref, gain_grad_ref):
    head = pl.program_id(0)

    @pl.when(head == 0)
    def _():
        low_small_ref[...] = jnp.zeros_like(low_small_ref)
        params_grad_ref[...] = jnp.zeros_like(params_grad_ref)
        gain_grad_ref[...] = jnp.zeros_like(gain_grad_ref)

    marks = marks_ref[...]
    pre = pre_ref[...]
    taps = taps_ref[...]
    tokens = pre.shape[0]
    total, gate, query_act, key_act, values, query_scale, key_scale = heads_inputs(pre, taps, marks, dk)
    queries = query_act * (query_scale * dk ** -0.5)
    keys = key_act * key_scale
    small = small_ref[...]
    params = params_ref[...]
    log_decay, beta = decays(small, params, head, heads)
    rows, cols = grids()
    gain = gain_ref[0:1]
    blocks = tokens // BLOCK
    upper = (rows <= cols).astype(BF)
    d_state = None
    d_query, d_key, d_value, d_beta, d_decay = [None] * blocks, [None] * blocks, [None] * blocks, [None] * blocks, [None] * blocks
    d_gain = jnp.zeros((1, dv), F32)
    for index in reversed(range(blocks)):
        at = slice(index * BLOCK, (index + 1) * BLOCK)
        grad = grad_ref[at, :]
        output = out_ref[at, :]
        gate_pre = pre[at, 2 * dk + dv :]
        gate_sig = sigmoid(gate_pre)
        gate_act = gate_pre * gate_sig
        scale = lax.rsqrt(jnp.mean(output * output, axis=1, keepdims=True) + 1e-05)
        normed = output * scale
        both = grad * normed
        d_gain = d_gain + jnp.sum(both * gate_act, axis=0, keepdims=True)
        low_ref[at, 2 * dk + dv :] = (
            both * gain * (gate_sig + gate_act * (1.0 - gate_sig))
        ).astype(BF)
        pulled = grad * gate_act * gain
        d_out = scale * (pulled - normed * jnp.mean(pulled * normed, axis=1, keepdims=True))

        seg_col, seg_row = marks[at, 6:7], segs_ref[0:1, at]
        last_seg = marks[index * BLOCK - 1 : index * BLOCK, 6:7] if index else None
        decay, carried = block_decay(log_decay[at], head, rows, cols, seg_col, seg_row, last_seg)
        key, query, value, strength = keys[at], queries[at], values[at], beta[at]
        inner, score, inverse = mats_ref[at, 0:BLOCK], mats_ref[at, BLOCK : 2 * BLOCK], mats_ref[at, 2 * BLOCK :]
        fresh_parts = split(fresh_ref[at, :])
        key_parts, query_parts = split(key), split(query)
        out_parts = split(d_out)
        d_fresh = dot3(split(score), out_parts, 0, 0)
        if d_state is not None:
            tail = lane_pick_row(decay)
            state_grad_parts = split(d_state)
            d_fresh = d_fresh + dot3(split(key * tail), state_grad_parts)
        d_source = dot3(split(inverse), split(d_fresh), 0, 0)
        source_parts = split(d_source)
        d_score = dot3(out_parts, fresh_parts, 1, 1)
        d_lower = jnp.where(rows > cols, -dot3(source_parts, fresh_parts, 1, 1), 0.0)
        d_value[index] = strength * d_source
        d_strength = jnp.sum(d_source * value, axis=1, keepdims=True) + jnp.sum(d_lower * inner, axis=1, keepdims=True)
        change = d_score * score + d_lower * (strength * inner)
        d_run = jnp.sum(change, axis=1, keepdims=True) - jnp.sum(change.T, axis=1, keepdims=True)
        d_scores = split(d_score * decay)
        d_inners = split(d_lower * (strength * decay))
        dq = dot3(d_scores, key_parts)
        dk_ = dot3(d_inners, key_parts) + dot3(d_inners, key_parts, 0, 0) + dot3(d_scores, query_parts, 0, 0)
        last_extra = None
        if d_state is not None:
            moved = dot3(fresh_parts, state_grad_parts, 1, 1)
            dk_ = dk_ + tail * moved
            d_tail = jnp.sum(key * moved, axis=1, keepdims=True) * tail
            d_run = d_run - d_tail
            last_extra = jnp.sum(d_tail, axis=0, keepdims=True)
        if index:
            state = states_ref[(index - 1) * dk : index * dk, :]
            state_parts = split(state)
            out_back = dot3(out_parts, state_parts, 1, 1)
            source_back = dot3(source_parts, state_parts, 1, 1)
            key_source = jnp.sum(key * source_back, axis=1, keepdims=True)
            d_carried = jnp.sum(query * out_back, axis=1, keepdims=True) - strength * key_source
            d_strength = d_strength - carried * key_source
            dq = dq + carried * out_back
            dk_ = dk_ - (strength * carried) * source_back
            d_run = d_run + d_carried * carried
            keep = carried[BLOCK - 1 : BLOCK]
            new_state = dot3(query_parts, split(carried * d_out), 0, 0) - dot3(
                key_parts, split((strength * carried) * d_source), 0, 0
            )
            if d_state is not None:
                kept = jnp.sum(jnp.sum(state * d_state, axis=1, keepdims=True), axis=0, keepdims=True)
                last_extra = last_extra + kept * keep
                new_state = new_state + keep * d_state
            d_state = new_state
        if last_extra is not None:
            at_last = lax.broadcasted_iota(jnp.int32, (BLOCK, 1), 0) == BLOCK - 1
            d_run = d_run + jnp.where(at_last, last_extra, 0.0)
        d_decay[index] = dotx(upper, jnp.broadcast_to(d_run, (BLOCK, BLOCK)))[:, 0:1]
        d_query[index], d_key[index], d_beta[index] = dq, dk_, d_strength

    dq = jnp.concatenate(d_query, axis=0) * dk ** -0.5
    dk_ = jnp.concatenate(d_key, axis=0)
    dv_ = jnp.concatenate(d_value, axis=0)
    query_pull = jnp.sum(dq * query_act, axis=1, keepdims=True)
    key_pull = jnp.sum(dk_ * key_act, axis=1, keepdims=True)
    d_query_act = query_scale * (dq - query_act * (query_scale * query_scale * query_pull))
    d_key_act = key_scale * (dk_ - key_act * (key_scale * key_scale * key_pull))
    d_act = jnp.concatenate([d_query_act, d_key_act, dv_], axis=1)
    d_total = d_act * (gate * (1.0 + total * (1.0 - gate)))
    x = pre[:, : taps.shape[1]]
    d_pre = d_total * taps[3:4]
    taps_grad_ref[3:4, :] = jnp.sum(d_total * x, axis=0, keepdims=True)
    for shift in (1, 2, 3):
        moved = marks[:, 2 + shift : 3 + shift] * pltpu.roll(d_total, tokens - shift, 0)
        d_pre = d_pre + moved * taps[3 - shift : 4 - shift]
        taps_grad_ref[3 - shift : 4 - shift, :] = jnp.sum(moved * x, axis=0, keepdims=True)
    low_ref[:, : taps.shape[1]] = d_pre.astype(BF)

    d_log = jnp.concatenate(d_decay, axis=0)
    d_str = jnp.concatenate(d_beta, axis=0)
    lane = lax.broadcasted_iota(jnp.int32, small.shape, 1)
    rate = jnp.exp(params[0:1])
    d_decay_pre = jnp.where(lane == head, d_log * (-rate) * sigmoid(small + params[1:2]), 0.0)
    d_beta_pre = jnp.where(lane == heads + head, d_str * beta * (1.0 - beta), 0.0)
    low_small_ref[...] += (d_decay_pre + d_beta_pre).astype(BF)
    params_grad_ref[0:1, :] += jnp.sum(jnp.where(lane == head, d_log * log_decay, 0.0), axis=0, keepdims=True)
    params_grad_ref[1:2, :] += jnp.sum(d_decay_pre, axis=0, keepdims=True)
    gain_grad_ref[0:1, :] += d_gain


def mixer_specs(tokens, heads, dk, dv):
    wide = 2 * dk + 2 * dv
    taps = 2 * dk + dv
    return [
        pl.BlockSpec((tokens, wide), lambda h: (0, h)),
        pl.BlockSpec((tokens, 128), lambda h: (0, heads * wide // 128)),
        pl.BlockSpec((4, taps), lambda h: (0, h)),
        pl.BlockSpec((tokens, 8), lambda h: (0, 0)),
        pl.BlockSpec((8, tokens), lambda h: (0, 0)),
        pl.BlockSpec((8, 128), lambda h: (0, 0)),
        pl.BlockSpec((8, dv), lambda h: (0, 0)),
    ]


def saved_specs(tokens, dk, dv):
    blocks = tokens // BLOCK
    return [
        pl.BlockSpec((tokens, dv), lambda h: (0, h)),
        pl.BlockSpec((tokens, dv), lambda h: (0, h)),
        pl.BlockSpec((tokens, 3 * BLOCK), lambda h: (0, h)),
        pl.BlockSpec(((blocks - 1) * dk, dv), lambda h: (0, h)),
    ]


def mixer_forward(tokens, heads, dk, dv, operands):
    blocks = tokens // BLOCK
    return pl.pallas_call(
        functools.partial(forward_kernel, heads, dk, dv),
        grid=(heads,),
        in_specs=mixer_specs(tokens, heads, dk, dv),
        out_specs=[pl.BlockSpec((tokens, dv), lambda h: (0, h))] + saved_specs(tokens, dk, dv),
        out_shape=[
            jax.ShapeDtypeStruct((tokens, heads * dv), BF),
            jax.ShapeDtypeStruct((tokens, heads * dv), F32),
            jax.ShapeDtypeStruct((tokens, heads * dv), F32),
            jax.ShapeDtypeStruct((tokens, heads * 3 * BLOCK), F32),
            jax.ShapeDtypeStruct(((blocks - 1) * dk, heads * dv), F32),
        ],
        compiler_params=pltpu.CompilerParams(vmem_limit_bytes=VMEM),
        name="mixer_forward",
    )(*operands)


def mixer_backward(tokens, heads, dk, dv, operands, grad, saved):
    wide = 2 * dk + 2 * dv
    taps = 2 * dk + dv
    return pl.pallas_call(
        functools.partial(backward_kernel, heads, dk, dv),
        grid=(heads,),
        in_specs=mixer_specs(tokens, heads, dk, dv)
        + [pl.BlockSpec((tokens, dv), lambda h: (0, h))]
        + saved_specs(tokens, dk, dv),
        out_specs=[
            pl.BlockSpec((tokens, wide), lambda h: (0, h)),
            pl.BlockSpec((tokens, 128), lambda h: (0, 0)),
            pl.BlockSpec((4, taps), lambda h: (0, h)),
            pl.BlockSpec((8, 128), lambda h: (0, 0)),
            pl.BlockSpec((8, dv), lambda h: (0, 0)),
        ],
        out_shape=[
            jax.ShapeDtypeStruct((tokens, heads * wide), BF),
            jax.ShapeDtypeStruct((tokens, 128), BF),
            jax.ShapeDtypeStruct((4, heads * taps), F32),
            jax.ShapeDtypeStruct((8, 128), F32),
            jax.ShapeDtypeStruct((8, dv), F32),
        ],
        compiler_params=pltpu.CompilerParams(vmem_limit_bytes=VMEM),
        name="mixer_backward",
    )(*operands, grad, *saved)


def wide_dot(left, right):
    return jnp.dot(left, right, preferred_element_type=F32)


def contract_tokens(left, right):
    return dot(left, right, 0, 0)


def contract_features(left, right):
    return dot(left, right, 1, 1)


def hop(values, step, size):
    return lax.ppermute(values, "col", [(at, (at + step) % size) for at in range(size)])


def gather_cols(values, place, size):
    width = values.shape[1]
    whole = jnp.zeros((values.shape[0], size * width), values.dtype)
    whole = lax.dynamic_update_slice(whole, values, (0, place * width))
    for step in range(1, size):
        origin = (place + size - step) % size
        whole = lax.dynamic_update_slice(whole, hop(values, step, size), (0, origin * width))
    return whole


def scatter_cols(partial_sum, place, size):
    rows, width = partial_sum.shape[0], partial_sum.shape[1] // size
    total = lax.dynamic_slice(partial_sum, (0, place * width), (rows, width))
    for step in range(1, size):
        target = (place + step) % size
        block = lax.dynamic_slice(partial_sum, (0, target * width), (rows, width)).astype(BF)
        total = total + hop(block, step, size).astype(F32)
    return total


def total_cols(values, size):
    total = values
    for step in range(1, size):
        total = total + hop(values, step, size)
    return total


def by_head(arrays, heads):
    lead = arrays[0].shape[0]
    return jnp.concatenate([a.reshape(lead, heads, -1) for a in arrays], axis=2).reshape(lead, -1)


def per_device(
    inputs,
    segment_ids,
    norm_gain,
    query_weight,
    key_weight,
    value_weight,
    gate_weight,
    decay_weight,
    beta_weight,
    query_conv,
    key_conv,
    value_conv,
    decay_log,
    decay_bias,
    head_gain,
    out_weight,
    second_gain,
    hidden_gate,
    hidden_up,
    hidden_down,
    cotangent,
):
    tokens, width = inputs.shape
    size = lax.axis_size("col")
    place = lax.axis_index("col")
    model = size * width
    heads = decay_weight.shape[1]
    dk = query_weight.shape[1] // heads
    dv = value_weight.shape[1] // heads
    depth = query_weight.shape[0]
    hidden_units = hidden_gate.shape[1]
    wide = 2 * dk + 2 * dv

    in_weight = jnp.concatenate(
        [
            by_head([query_weight, key_weight, value_weight, gate_weight], heads),
            decay_weight,
            beta_weight,
            jnp.zeros((depth, 128 - 2 * heads), BF),
        ],
        axis=1,
    )
    in_all = lax.all_gather(in_weight, "row", axis=0, tiled=True)
    out_all = lax.all_gather(out_weight, "row", axis=1, tiled=True)
    mlp_all = lax.all_gather(jnp.concatenate([hidden_gate, hidden_up], axis=1), "row", axis=0, tiled=True)
    down_all = lax.all_gather(hidden_down, "row", axis=1, tiled=True)

    inputs_all = gather_cols(inputs, place, size)
    gains_all = gather_cols(jnp.stack([norm_gain, second_gain]), place, size)
    grad_all = gather_cols(cotangent, place, size)

    wide_all = inputs_all.astype(F32)
    first_scale = lax.rsqrt(jnp.mean(wide_all * wide_all, axis=1, keepdims=True) + 1e-05)
    hidden = (wide_all * first_scale * gains_all[0:1]).astype(BF)
    pre = wide_dot(hidden, in_all)

    times = jnp.arange(tokens)
    marks = [
        jnp.where((times >= shift) & (jnp.roll(segment_ids, shift) == segment_ids), 1.0, 0.0) for shift in (1, 2, 3)
    ]
    marks = marks + [jnp.roll(mark, -shift) for mark, shift in zip(marks, (1, 2, 3))]
    seg = segment_ids.astype(F32)
    marks = jnp.stack(marks + [seg, seg], axis=1)
    segs = jnp.broadcast_to(seg[None], (8, tokens))
    params = jnp.pad(jnp.stack([decay_log, decay_bias]), ((0, 6), (0, 128 - heads)))
    gain = jnp.broadcast_to(head_gain[None], (8, dv))
    taps = by_head([query_conv, key_conv, value_conv], heads)
    operands = (pre, pre, taps, marks, segs, params, gain)
    mixed, *saved = mixer_forward(tokens, heads, dk, dv, operands)

    wide_inputs = inputs.astype(F32)
    residual = wide_inputs + scatter_cols(wide_dot(mixed, out_all), place, size)
    residual_all = gather_cols(residual.astype(BF), place, size).astype(F32)
    second_scale = lax.rsqrt(jnp.mean(residual_all * residual_all, axis=1, keepdims=True) + 1e-05)
    second = (residual_all * second_scale * gains_all[1:2]).astype(BF)
    both = wide_dot(second, mlp_all)
    gate_value, up_value = both[:, :hidden_units], both[:, hidden_units:]
    gate_sig = jax.nn.sigmoid(gate_value)
    gate_act = gate_value * gate_sig
    product = (gate_act * up_value).astype(BF)
    grad_product = contract_features(grad_all, down_all)
    grad_both = jnp.concatenate(
        [grad_product * up_value * (gate_sig * (1.0 + gate_value * (1.0 - gate_sig))), grad_product * gate_act], axis=1
    ).astype(BF)
    second_part = contract_features(grad_both, mlp_all)
    second_inner = total_cols(jnp.sum(second_part * gains_all[1:2] * residual_all, axis=1), size)[:, None]
    grad_second = scatter_cols(second_part, place, size)
    grad_residual = (
        cotangent.astype(F32)
        + second_scale * second_gain * grad_second
        - residual * (second_scale * second_scale * second_scale * second_inner / model)
    )
    second_gain_part = jnp.sum(grad_second * residual * second_scale, axis=0)
    residual_rows = gather_cols(grad_residual.astype(BF), place, size)
    grad_mixed = contract_features(residual_rows, out_all)
    low, low_small, taps_part, params_part, gain_part = mixer_backward(
        tokens, heads, dk, dv, operands, grad_mixed, saved
    )
    low_all = jnp.concatenate([low, low_small], axis=1)
    in_part = contract_tokens(hidden, low_all).astype(BF)
    hidden_part = contract_features(low_all, in_all)
    first_inner = total_cols(jnp.sum(hidden_part * gains_all[0:1] * wide_all, axis=1), size)[:, None]
    grad_hidden = scatter_cols(hidden_part, place, size)
    grad_inputs = (
        grad_residual
        + first_scale * norm_gain * grad_hidden
        - wide_inputs * (first_scale * first_scale * first_scale * first_inner / model)
    )
    first_gain_part = jnp.sum(grad_hidden * wide_inputs * first_scale, axis=0)

    result = residual + scatter_cols(wide_dot(product, down_all), place, size)
    down_part = contract_tokens(product, grad_all).astype(BF)
    mlp_part = contract_tokens(second, grad_both).astype(BF)
    out_part = contract_tokens(mixed, residual_rows).astype(BF)
    down_grad = lax.psum_scatter(down_part, "row", scatter_dimension=1, tiled=True).astype(F32)
    mlp_grad = lax.psum_scatter(mlp_part, "row", scatter_dimension=0, tiled=True).astype(F32)
    out_grad = lax.psum_scatter(out_part, "row", scatter_dimension=1, tiled=True).astype(F32)
    in_grad = lax.psum_scatter(in_part, "row", scatter_dimension=0, tiled=True).astype(F32)

    taps_grad, params_grad, second_gain_grad = lax.psum(
        (taps_part, params_part[0:2, :heads], second_gain_part), "row"
    )
    gain_grad = lax.psum(gain_part[0], ("row", "col"))
    norm_gain_grad = lax.psum(first_gain_part, "row")

    head_grads = in_grad[:, : heads * wide].reshape(depth, heads, wide)
    tap_grads = taps_grad.reshape(4, heads, 2 * dk + dv)
    return (
        result,
        grad_inputs,
        norm_gain_grad,
        head_grads[:, :, :dk].reshape(depth, -1),
        head_grads[:, :, dk : 2 * dk].reshape(depth, -1),
        head_grads[:, :, 2 * dk : 2 * dk + dv].reshape(depth, -1),
        head_grads[:, :, 2 * dk + dv :].reshape(depth, -1),
        in_grad[:, heads * wide : heads * wide + heads],
        in_grad[:, heads * wide + heads : heads * wide + 2 * heads],
        tap_grads[:, :, :dk].reshape(4, -1),
        tap_grads[:, :, dk : 2 * dk].reshape(4, -1),
        tap_grads[:, :, 2 * dk :].reshape(4, -1),
        params_grad[0],
        params_grad[1],
        gain_grad,
        out_grad,
        second_gain_grad,
        mlp_grad[:, :hidden_units],
        mlp_grad[:, hidden_units:],
        down_grad,
    )


ROW_COL = P("row", "col")
COL_ROW = P("col", "row")
PLACED = (
    ROW_COL, P("row"), P("col"),
    ROW_COL, ROW_COL, ROW_COL, ROW_COL, ROW_COL, ROW_COL,
    P(None, "col"), P(None, "col"), P(None, "col"),
    P("col"), P("col"), P(),
    COL_ROW, P("col"), ROW_COL, ROW_COL, COL_ROW, ROW_COL,
)
MADE = (
    ROW_COL, ROW_COL, P("col"),
    ROW_COL, ROW_COL, ROW_COL, ROW_COL, ROW_COL, ROW_COL,
    P(None, "col"), P(None, "col"), P(None, "col"),
    P("col"), P("col"), P(),
    COL_ROW, P("col"), ROW_COL, ROW_COL, COL_ROW,
)


def solution(mesh):
    return jax.shard_map(per_device, mesh=mesh, in_specs=PLACED, out_specs=MADE, check_vma=False)
```

```python
import functools
import jax
import jax.numpy as jnp
from jax import lax
from jax.experimental import pallas as pl
from jax.experimental.pallas import tpu as pltpu
from jax.sharding import PartitionSpec as P

BF = jnp.bfloat16
F32 = jnp.float32
BLOCK = 128
COST = pl.CostEstimate(flops=20_000_000_000, bytes_accessed=20_000_000, transcendentals=4_000_000)
VMEM = 56 * 1024 * 1024


def dot(left, right, lc=1, rc=0):
    return lax.dot_general(left, right, (((lc,), (rc,)), ((), ())), preferred_element_type=F32)


def split(x):
    high = x.astype(BF)
    return high, (x - high.astype(F32)).astype(BF)


def dot3(left, right, lc=1, rc=0):
    return (
        dot(left[0], right[0], lc, rc) + dot(left[0], right[1], lc, rc) + dot(left[1], right[0], lc, rc)
    )


def dotx(left, right, lc=1, rc=0):
    first = right.astype(BF)
    rest = right - first.astype(F32)
    second = rest.astype(BF)
    third = (rest - second.astype(F32)).astype(BF)
    return dot(left, first, lc, rc) + dot(left, second, lc, rc) + dot(left, third, lc, rc)


def sigmoid(x):
    return 0.5 + 0.5 * jnp.tanh(0.5 * x)


def lane_pick(block, lane):
    index = lax.broadcasted_iota(jnp.int32, block.shape, 1)
    return jnp.sum(jnp.where(index == lane, block, 0.0), axis=1, keepdims=True)


def row_pick(block, row):
    index = lax.broadcasted_iota(jnp.int32, block.shape, 0)
    return jnp.sum(jnp.where(index == row, block, 0.0), axis=0, keepdims=True)


def softplus(x):
    return jnp.maximum(x, 0.0) + jnp.log1p(jnp.exp(-jnp.abs(x)))


def conv_act(x, taps, marks):
    total = x * taps[3:4]
    for shift in (1, 2, 3):
        total = total + (marks[:, shift - 1 : shift] * pltpu.roll(x, shift, 0)) * taps[3 - shift : 4 - shift]
    gate = sigmoid(total)
    return total, gate


def grids():
    rows = lax.broadcasted_iota(jnp.int32, (BLOCK, BLOCK), 0)
    cols = lax.broadcasted_iota(jnp.int32, (BLOCK, BLOCK), 1)
    return rows, cols


def decays(small, params, head, heads):
    rate = jnp.exp(params[0:1])
    log_decay = -rate * softplus(small + params[1:2])
    beta = sigmoid(lane_pick(small, heads + head))
    return log_decay, beta


def block_decay(log_decay, head, rows, cols, seg_col, seg_row, last_seg):
    lower = (rows >= cols).astype(BF)
    running = dotx(lower, log_decay)
    column = lane_pick(running, head)
    line = row_pick(running.T, head)
    same = (seg_col == seg_row) & (rows >= cols)
    decay = jnp.where(same, jnp.exp(jnp.minimum(column - line, 0.0)), 0.0)
    carried = None
    if last_seg is not None:
        carried = jnp.where(seg_col == last_seg, jnp.exp(column), 0.0)
    return decay, carried


def unit_inverses(lowers, rows, cols):
    identity = (rows == cols).astype(F32)
    base = 16
    same = (rows // base) == (cols // base)
    nears = [jnp.where(same, -lower, 0.0) for lower in lowers]
    powers = [split(near) for near in nears]
    totals = [identity + near for near in nears]
    width = 2
    while width < base:
        powers = [split(dot3(power, power)) for power in powers]
        totals = [total + dot3(split(total), power) for total, power in zip(totals, powers)]
        width *= 2
    while base < BLOCK:
        pair_at = (rows // (2 * base) == cols // (2 * base)) & (rows // base != cols // base)
        offs = [split(jnp.where(pair_at, lower, 0.0)) for lower in lowers]
        parts = [split(total) for total in totals]
        middles = [split(dot3(off, part)) for off, part in zip(offs, parts)]
        totals = [total - dot3(part, middle) for total, part, middle in zip(totals, parts, middles)]
        base *= 2
    return totals


def head_inputs(pres, taps_refs, marks):
    query_taps, key_taps, value_taps = taps_refs
    dk = pres[0].shape[1]
    x = jnp.concatenate(pres, axis=1)
    taps = jnp.concatenate([query_taps[...], key_taps[...], value_taps[...]], axis=1)
    total, gate = conv_act(x, taps, marks)
    act = total * gate
    query_act, key_act, values = act[:, :dk], act[:, dk : 2 * dk], act[:, 2 * dk :]
    query_scale = lax.rsqrt(jnp.sum(query_act * query_act, axis=1, keepdims=True) + 1e-06)
    key_scale = lax.rsqrt(jnp.sum(key_act * key_act, axis=1, keepdims=True) + 1e-06)
    return x, taps, total, gate, query_act, key_act, values, query_scale, key_scale


def forward_kernel(heads, hidden_ref, query_weight, key_weight, value_weight, gate_weight, small_weight,
                   query_taps, key_taps, value_taps, marks_ref, segs_ref, params_ref, gain_ref,
                   query_ref, key_ref, value_ref, gate_ref, small_ref,
                   mixed_ref, out_ref, fresh_ref, mats_ref, states_ref):
    head = pl.program_id(0)
    hidden = hidden_ref[...]

    @pl.when(head == 0)
    def _():
        small_ref[...] = dot(hidden, small_weight[...])

    query_ref[...] = dot(hidden, query_weight[...])
    key_ref[...] = dot(hidden, key_weight[...])
    value_ref[...] = dot(hidden, value_weight[...])
    gate_ref[...] = dot(hidden, gate_weight[...])
    marks = marks_ref[...]
    _, _, _, _, query_act, key_act, values, query_scale, key_scale = head_inputs(
        [query_ref[...], key_ref[...], value_ref[...]], (query_taps, key_taps, value_taps), marks
    )
    tokens, dk = query_act.shape
    queries = query_act * (query_scale * dk ** -0.5)
    keys = key_act * key_scale
    log_decay, beta = decays(small_ref[...], params_ref[...], head, heads)
    rows, cols = grids()
    blocks = tokens // BLOCK
    cuts = [slice(index * BLOCK, (index + 1) * BLOCK) for index in range(blocks)]
    key_parts = [split(keys[at]) for at in cuts]
    query_parts = [split(queries[at]) for at in cuts]
    decay_pairs = [
        block_decay(
            log_decay[at], head, rows, cols, marks[at, 6:7], segs_ref[0:1, at],
            marks[index * BLOCK - 1 : index * BLOCK, 6:7] if index else None,
        )
        for index, at in enumerate(cuts)
    ]
    inners = [
        jnp.where(rows > cols, dot3(key, key, 1, 1) * pair_of[0], 0.0) for key, pair_of in zip(key_parts, decay_pairs)
    ]
    scores = [dot3(query, key, 1, 1) * pair_of[0] for query, key, pair_of in zip(query_parts, key_parts, decay_pairs)]
    inverses = unit_inverses([beta[at] * inner for at, inner in zip(cuts, inners)], rows, cols)
    state = None
    for index, at in enumerate(cuts):
        decay, carried = decay_pairs[index]
        inner, score, inverse = inners[index], scores[index], inverses[index]
        value, strength = values[at], beta[at]
        mats_ref[at, 0:BLOCK] = inner
        mats_ref[at, BLOCK : 2 * BLOCK] = score
        mats_ref[at, 2 * BLOCK :] = inverse
        if index:
            state_parts = split(state)
            source = strength * (value - carried * dot3(key_parts[index], state_parts))
        else:
            source = strength * value
        fresh = dot3(split(inverse), split(source))
        fresh_parts = split(fresh)
        output = dot3(split(score), fresh_parts)
        if index:
            output = output + carried * dot3(query_parts[index], state_parts)
        if index + 1 < blocks:
            grown = dot3(split(keys[at] * lane_pick_row(decay)), fresh_parts, 0, 0)
            state = grown if state is None else carried[BLOCK - 1 : BLOCK] * state + grown
            states_ref[index * dk : (index + 1) * dk, :] = state
        fresh_ref[at, :] = fresh
        out_ref[at, :] = output
        scale = lax.rsqrt(jnp.mean(output * output, axis=1, keepdims=True) + 1e-05)
        gate_pre = gate_ref[at, :]
        mixed_ref[at, :] = (output * scale * gain_ref[0:1] * (gate_pre * sigmoid(gate_pre))).astype(BF)


def lane_pick_row(decay):
    return decay.T[:, BLOCK - 1 : BLOCK]


def backward_kernel(heads, first, query_ref, key_ref, value_ref, gate_ref, small_ref, query_taps, key_taps, value_taps,
                    marks_ref, segs_ref, params_ref, gain_ref, grad_ref, out_ref, fresh_ref, mats_ref, states_ref,
                    low_query_ref, low_key_ref, low_value_ref, low_gate_ref, low_small_ref,
                    query_taps_grad, key_taps_grad, value_taps_grad, params_grad_ref, gain_grad_ref):
    head = first + pl.program_id(0)

    @pl.when(pl.program_id(0) == 0)
    def _():
        low_small_ref[...] = jnp.zeros_like(low_small_ref)
        params_grad_ref[...] = jnp.zeros_like(params_grad_ref)
        gain_grad_ref[...] = jnp.zeros_like(gain_grad_ref)

    marks = marks_ref[...]
    x, taps, total, gate, query_act, key_act, values, query_scale, key_scale = head_inputs(
        [query_ref[...], key_ref[...], value_ref[...]], (query_taps, key_taps, value_taps), marks
    )
    tokens, dk = query_act.shape
    dv = values.shape[1]
    queries = query_act * (query_scale * dk ** -0.5)
    keys = key_act * key_scale
    small = small_ref[...]
    params = params_ref[...]
    log_decay, beta = decays(small, params, head, heads)
    rows, cols = grids()
    gain = gain_ref[0:1]
    blocks = tokens // BLOCK
    upper = (rows <= cols).astype(BF)
    d_state = None
    d_query, d_key, d_value, d_beta, d_decay = [None] * blocks, [None] * blocks, [None] * blocks, [None] * blocks, [None] * blocks
    d_gain = jnp.zeros((1, dv), F32)
    for index in reversed(range(blocks)):
        at = slice(index * BLOCK, (index + 1) * BLOCK)
        grad = grad_ref[at, :]
        output = out_ref[at, :]
        gate_pre = gate_ref[at, :]
        gate_sig = sigmoid(gate_pre)
        gate_act = gate_pre * gate_sig
        scale = lax.rsqrt(jnp.mean(output * output, axis=1, keepdims=True) + 1e-05)
        normed = output * scale
        both = grad * normed
        d_gain = d_gain + jnp.sum(both * gate_act, axis=0, keepdims=True)
        low_gate_ref[at, :] = (
            both * gain * (gate_sig + gate_act * (1.0 - gate_sig))
        ).astype(BF)
        pulled = grad * gate_act * gain
        d_out = scale * (pulled - normed * jnp.mean(pulled * normed, axis=1, keepdims=True))

        seg_col, seg_row = marks[at, 6:7], segs_ref[0:1, at]
        last_seg = marks[index * BLOCK - 1 : index * BLOCK, 6:7] if index else None
        decay, carried = block_decay(log_decay[at], head, rows, cols, seg_col, seg_row, last_seg)
        key, query, value, strength = keys[at], queries[at], values[at], beta[at]
        inner, score, inverse = mats_ref[at, 0:BLOCK], mats_ref[at, BLOCK : 2 * BLOCK], mats_ref[at, 2 * BLOCK :]
        fresh_parts = split(fresh_ref[at, :])
        key_parts, query_parts = split(key), split(query)
        out_parts = split(d_out)
        d_fresh = dot3(split(score), out_parts, 0, 0)
        if d_state is not None:
            tail = lane_pick_row(decay)
            state_grad_parts = split(d_state)
            d_fresh = d_fresh + dot3(split(key * tail), state_grad_parts)
        d_source = dot3(split(inverse), split(d_fresh), 0, 0)
        source_parts = split(d_source)
        d_score = dot3(out_parts, fresh_parts, 1, 1)
        d_lower = jnp.where(rows > cols, -dot3(source_parts, fresh_parts, 1, 1), 0.0)
        d_value[index] = strength * d_source
        d_strength = jnp.sum(d_source * value, axis=1, keepdims=True) + jnp.sum(d_lower * inner, axis=1, keepdims=True)
        change = d_score * score + d_lower * (strength * inner)
        d_run = jnp.sum(change, axis=1, keepdims=True) - jnp.sum(change.T, axis=1, keepdims=True)
        d_scores = split(d_score * decay)
        d_inners = split(d_lower * (strength * decay))
        dq = dot3(d_scores, key_parts)
        dk_ = dot3(d_inners, key_parts) + dot3(d_inners, key_parts, 0, 0) + dot3(d_scores, query_parts, 0, 0)
        last_extra = None
        if d_state is not None:
            moved = dot3(fresh_parts, state_grad_parts, 1, 1)
            dk_ = dk_ + tail * moved
            d_tail = jnp.sum(key * moved, axis=1, keepdims=True) * tail
            d_run = d_run - d_tail
            last_extra = jnp.sum(d_tail, axis=0, keepdims=True)
        if index:
            state = states_ref[(index - 1) * dk : index * dk, :]
            state_parts = split(state)
            out_back = dot3(out_parts, state_parts, 1, 1)
            source_back = dot3(source_parts, state_parts, 1, 1)
            key_source = jnp.sum(key * source_back, axis=1, keepdims=True)
            d_carried = jnp.sum(query * out_back, axis=1, keepdims=True) - strength * key_source
            d_strength = d_strength - carried * key_source
            dq = dq + carried * out_back
            dk_ = dk_ - (strength * carried) * source_back
            d_run = d_run + d_carried * carried
            keep = carried[BLOCK - 1 : BLOCK]
            new_state = dot3(query_parts, split(carried * d_out), 0, 0) - dot3(
                key_parts, split((strength * carried) * d_source), 0, 0
            )
            if d_state is not None:
                kept = jnp.sum(jnp.sum(state * d_state, axis=1, keepdims=True), axis=0, keepdims=True)
                last_extra = last_extra + kept * keep
                new_state = new_state + keep * d_state
            d_state = new_state
        if last_extra is not None:
            at_last = lax.broadcasted_iota(jnp.int32, (BLOCK, 1), 0) == BLOCK - 1
            d_run = d_run + jnp.where(at_last, last_extra, 0.0)
        d_decay[index] = dotx(upper, jnp.broadcast_to(d_run, (BLOCK, BLOCK)))[:, 0:1]
        d_query[index], d_key[index], d_beta[index] = dq, dk_, d_strength

    dq = jnp.concatenate(d_query, axis=0) * dk ** -0.5
    dk_ = jnp.concatenate(d_key, axis=0)
    dv_ = jnp.concatenate(d_value, axis=0)
    query_pull = jnp.sum(dq * query_act, axis=1, keepdims=True)
    key_pull = jnp.sum(dk_ * key_act, axis=1, keepdims=True)
    d_query_act = query_scale * (dq - query_act * (query_scale * query_scale * query_pull))
    d_key_act = key_scale * (dk_ - key_act * (key_scale * key_scale * key_pull))
    d_act = jnp.concatenate([d_query_act, d_key_act, dv_], axis=1)
    d_total = d_act * (gate * (1.0 + total * (1.0 - gate)))
    d_pre = d_total * taps[3:4]
    tap_sums = [None, None, None, jnp.sum(d_total * x, axis=0, keepdims=True)]
    for shift in (1, 2, 3):
        moved = marks[:, 2 + shift : 3 + shift] * pltpu.roll(d_total, tokens - shift, 0)
        d_pre = d_pre + moved * taps[3 - shift : 4 - shift]
        tap_sums[3 - shift] = jnp.sum(moved * x, axis=0, keepdims=True)
    d_pre = d_pre.astype(BF)
    low_query_ref[...] = d_pre[:, :dk]
    low_key_ref[...] = d_pre[:, dk : 2 * dk]
    low_value_ref[...] = d_pre[:, 2 * dk :]
    for tap in range(4):
        query_taps_grad[tap : tap + 1, :] = tap_sums[tap][:, :dk]
        key_taps_grad[tap : tap + 1, :] = tap_sums[tap][:, dk : 2 * dk]
        value_taps_grad[tap : tap + 1, :] = tap_sums[tap][:, 2 * dk :]

    d_log = jnp.concatenate(d_decay, axis=0)
    d_str = jnp.concatenate(d_beta, axis=0)
    lane = lax.broadcasted_iota(jnp.int32, small.shape, 1)
    rate = jnp.exp(params[0:1])
    d_decay_pre = jnp.where(lane == head, d_log * (-rate) * sigmoid(small + params[1:2]), 0.0)
    d_beta_pre = jnp.where(lane == heads + head, d_str * beta * (1.0 - beta), 0.0)
    low_small_ref[...] += (d_decay_pre + d_beta_pre).astype(BF)
    params_grad_ref[0:1, :] += jnp.sum(jnp.where(lane == head, d_log * log_decay, 0.0), axis=0, keepdims=True)
    params_grad_ref[1:2, :] += jnp.sum(d_decay_pre, axis=0, keepdims=True)
    gain_grad_ref[0:1, :] += d_gain


def whole(h):
    return (0, 0)


def of_head(first):
    return lambda h: (0, first + h)


def shared_specs(tokens, dk, dv, first):
    own = of_head(first)
    return [
        pl.BlockSpec((4, dk), own),
        pl.BlockSpec((4, dk), own),
        pl.BlockSpec((4, dv), own),
        pl.BlockSpec((tokens, 8), whole),
        pl.BlockSpec((8, tokens), whole),
        pl.BlockSpec((8, 128), whole),
        pl.BlockSpec((8, dv), whole),
    ]


def pre_specs(tokens, dk, dv, first):
    own = of_head(first)
    return [
        pl.BlockSpec((tokens, dk), own),
        pl.BlockSpec((tokens, dk), own),
        pl.BlockSpec((tokens, dv), own),
        pl.BlockSpec((tokens, dv), own),
        pl.BlockSpec((tokens, 128), whole),
    ]


def saved_specs(tokens, dk, dv, first):
    own = of_head(first)
    blocks = tokens // BLOCK
    return [
        pl.BlockSpec((tokens, dv), own),
        pl.BlockSpec((tokens, dv), own),
        pl.BlockSpec((tokens, 3 * BLOCK), own),
        pl.BlockSpec(((blocks - 1) * dk, dv), own),
    ]


def mixer_forward(heads, dk, dv, hidden, weight, shared):
    tokens, model = hidden.shape
    blocks = tokens // BLOCK
    each = heads // 2
    wide = 2 * dk + 2 * dv

    def columns(size, before):
        return lambda h: (0, (h // each * each * wide + each * before) // size + h % each)

    return pl.pallas_call(
        functools.partial(forward_kernel, heads),
        grid=(heads,),
        in_specs=[
            pl.BlockSpec((tokens, model), whole),
            pl.BlockSpec((model, dk), columns(dk, 0)),
            pl.BlockSpec((model, dk), columns(dk, dk)),
            pl.BlockSpec((model, dv), columns(dv, 2 * dk)),
            pl.BlockSpec((model, dv), columns(dv, 2 * dk + dv)),
            pl.BlockSpec((model, 128), lambda h: (0, heads * wide // 128)),
        ]
        + shared_specs(tokens, dk, dv, 0),
        out_specs=pre_specs(tokens, dk, dv, 0)
        + [pl.BlockSpec((tokens, dv), of_head(0))]
        + saved_specs(tokens, dk, dv, 0),
        out_shape=[
            jax.ShapeDtypeStruct((tokens, heads * dk), F32),
            jax.ShapeDtypeStruct((tokens, heads * dk), F32),
            jax.ShapeDtypeStruct((tokens, heads * dv), F32),
            jax.ShapeDtypeStruct((tokens, heads * dv), F32),
            jax.ShapeDtypeStruct((tokens, 128), F32),
            jax.ShapeDtypeStruct((tokens, heads * dv), BF),
            jax.ShapeDtypeStruct((tokens, heads * dv), F32),
            jax.ShapeDtypeStruct((tokens, heads * dv), F32),
            jax.ShapeDtypeStruct((tokens, heads * 3 * BLOCK), F32),
            jax.ShapeDtypeStruct(((blocks - 1) * dk, heads * dv), F32),
        ],
        compiler_params=pltpu.CompilerParams(vmem_limit_bytes=VMEM),
        cost_estimate=COST,
        name="mixer_forward",
    )(hidden, weight, weight, weight, weight, weight, *shared)


def mixer_backward(heads, dk, dv, pres, shared, grad, saved, first, count):
    tokens = grad.shape[0]
    own = of_head(0)
    return pl.pallas_call(
        functools.partial(backward_kernel, heads, first),
        grid=(count,),
        in_specs=pre_specs(tokens, dk, dv, first)
        + shared_specs(tokens, dk, dv, first)
        + [pl.BlockSpec((tokens, dv), of_head(first))]
        + saved_specs(tokens, dk, dv, first),
        out_specs=[
            pl.BlockSpec((tokens, dk), own),
            pl.BlockSpec((tokens, dk), own),
            pl.BlockSpec((tokens, dv), own),
            pl.BlockSpec((tokens, dv), own),
            pl.BlockSpec((tokens, 128), whole),
            pl.BlockSpec((4, dk), own),
            pl.BlockSpec((4, dk), own),
            pl.BlockSpec((4, dv), own),
            pl.BlockSpec((8, 128), whole),
            pl.BlockSpec((8, dv), whole),
        ],
        out_shape=[
            jax.ShapeDtypeStruct((tokens, count * dk), BF),
            jax.ShapeDtypeStruct((tokens, count * dk), BF),
            jax.ShapeDtypeStruct((tokens, count * dv), BF),
            jax.ShapeDtypeStruct((tokens, count * dv), BF),
            jax.ShapeDtypeStruct((tokens, 128), BF),
            jax.ShapeDtypeStruct((4, count * dk), F32),
            jax.ShapeDtypeStruct((4, count * dk), F32),
            jax.ShapeDtypeStruct((4, count * dv), F32),
            jax.ShapeDtypeStruct((8, 128), F32),
            jax.ShapeDtypeStruct((8, dv), F32),
        ],
        compiler_params=pltpu.CompilerParams(vmem_limit_bytes=VMEM),
        cost_estimate=COST,
        name="mixer_backward",
    )(*pres, *shared, grad, *saved)


def wide_dot(left, right):
    return jnp.dot(left, right, preferred_element_type=F32)


def contract_tokens(left, right):
    return dot(left, right, 0, 0)


def contract_features(left, right):
    return dot(left, right, 1, 1)


def after(values, *first):
    return lax.optimization_barrier((values, first))[0]


def fence(*values):
    return lax.optimization_barrier(values)


def hop(values, step, size):
    return lax.ppermute(values, "col", [(at, (at + step) % size) for at in range(size)])


def hops(values, size):
    return [values] + [hop(values, step, size) for step in range(1, size)]


def lay(pieces, spots, width):
    whole = jnp.zeros((pieces[0].shape[0], len(pieces) * width), pieces[0].dtype)
    for piece, spot in zip(pieces, spots):
        whole = lax.dynamic_update_slice(whole, piece, (0, spot * width))
    return whole


def gather_cols(values, place, size):
    return lay_cols(hops(values, size), place, size)


def lay_cols(pieces, place, size):
    return lay(pieces, [(place + size - step) % size for step in range(size)], pieces[0].shape[1])


def send_cols(pieces, size):
    return [hop(piece, step + 1, size) for step, piece in enumerate(pieces)]


def add_cols(own, received):
    for piece in received:
        own = own + piece.astype(F32)
    return own


def cut_cols(partial_sum, place, size):
    rows, width = partial_sum.shape[0], partial_sum.shape[1] // size
    own = lax.dynamic_slice(partial_sum, (0, place * width), (rows, width))
    return own, [
        lax.dynamic_slice(partial_sum, (0, (place + step) % size * width), (rows, width)).astype(BF)
        for step in range(1, size)
    ]


def pair(values, mask, rows):
    return lax.ppermute(values, "row", [(at, at ^ mask) for at in range(rows)])


def chips(rows):
    return rows == 8


def order_features(values, rows):
    if not chips(rows):
        return [values]
    here = lax.axis_index("row")
    depth = values.shape[1] // rows
    return [
        jnp.concatenate(
            [
                lax.dynamic_slice(values, (0, (here ^ chip ^ core) * depth), (values.shape[0], depth))
                for chip in (0, 2, 4, 6)
            ],
            axis=1,
        )
        for core in (0, 1)
    ]


def away_part(left, right, rows):
    return contract_tokens(left[1], right).astype(BF) if chips(rows) else None


def near_part(left, right, away, rows):
    if not chips(rows):
        return contract_tokens(left[0], right).astype(BF), None
    return (left[0], right), pair(away, 1, rows)


def hold(near, given, rows):
    return near if given is None else (contract_tokens(*near) + given.astype(F32)).astype(BF)


def send_chips(held, rows):
    if not chips(rows):
        return None, None
    depth = held.shape[0] // 4
    half = depth // 2
    own, x, y, far = (held[at * depth : (at + 1) * depth] for at in range(4))
    from_x = pair(jnp.concatenate([far[:half], x[:half]], axis=0), 2, rows)
    from_y = pair(jnp.concatenate([far[half:], y[half:]], axis=0), 4, rows)
    return from_x, from_y


def last_step(held, from_x, from_y, rows):
    if from_x is None:
        return lax.psum_scatter(held, "row", scatter_dimension=0, tiled=True), None, None, None
    depth = held.shape[0] // 4
    half = depth // 2
    own, x, y, far = (held[at * depth : (at + 1) * depth] for at in range(4))
    last_x = pair((x[half:].astype(F32) + from_y[:half].astype(F32)).astype(BF), 2, rows)
    last_y = pair((y[:half].astype(F32) + from_x[:half].astype(F32)).astype(BF), 4, rows)
    mine = own.astype(F32) + jnp.concatenate([from_x[half:], from_y[half:]], axis=0).astype(F32)
    return mine, last_x, last_y, rows


def finish(mine, last_x, last_y, rows):
    if last_x is None:
        return mine.astype(F32)
    return mine + jnp.concatenate([last_y, last_x], axis=0).astype(F32)


def per_device(
    inputs,
    segment_ids,
    norm_gain,
    query_weight,
    key_weight,
    value_weight,
    gate_weight,
    decay_weight,
    beta_weight,
    query_conv,
    key_conv,
    value_conv,
    decay_log,
    decay_bias,
    head_gain,
    out_weight,
    second_gain,
    hidden_gate,
    hidden_up,
    hidden_down,
    cotangent,
):
    tokens, width = inputs.shape
    size = lax.axis_size("col")
    rows = lax.axis_size("row")
    place = lax.axis_index("col")
    model = size * width
    heads = decay_weight.shape[1]
    dk = query_weight.shape[1] // heads
    dv = value_weight.shape[1] // heads
    depth = query_weight.shape[0]
    hidden_units = hidden_gate.shape[1]
    wide = 2 * dk + 2 * dv
    each = heads // 2
    span = each * wide

    def per_half(arrays, sizes):
        return [
            array[:, half * each * size : (half + 1) * each * size] for half in (0, 1) for array, size in zip(arrays, sizes)
        ]

    in_weight = jnp.concatenate(
        per_half([query_weight, key_weight, value_weight, gate_weight], [dk, dk, dv, dv])
        + [decay_weight, beta_weight, jnp.zeros((depth, 128 - 2 * heads), BF)],
        axis=1,
    )
    inputs_all = gather_cols(inputs, place, size)
    gains_all = gather_cols(jnp.stack([norm_gain, second_gain]), place, size)
    in_all = lax.all_gather(in_weight, "row", axis=0, tiled=True)
    out_all = lax.all_gather(out_weight, "row", axis=1, tiled=True)
    hidden_gate, hidden_up, hidden_down = after((hidden_gate, hidden_up, hidden_down), in_weight)
    stacked = jnp.concatenate([hidden_gate.T, hidden_up.T, hidden_down], axis=0)
    stacked = lax.all_gather(stacked, "row", axis=1, tiled=True)
    mlp_all, down_all = stacked[: 2 * hidden_units], stacked[2 * hidden_units :]
    first_gains, second_gains = gains_all[0:1], gains_all[1:2]

    wide_all = inputs_all.astype(F32)
    first_scale = lax.rsqrt(jnp.mean(wide_all * wide_all, axis=1, keepdims=True) + 1e-05)
    hidden, in_all, cotangent_late = fence((wide_all * first_scale * first_gains).astype(BF), in_all, cotangent)
    grad_all = gather_cols(cotangent_late, place, size)

    times = jnp.arange(tokens)
    marks = [
        jnp.where((times >= shift) & (jnp.roll(segment_ids, shift) == segment_ids), 1.0, 0.0) for shift in (1, 2, 3)
    ]
    marks = marks + [jnp.roll(mark, -shift) for mark, shift in zip(marks, (1, 2, 3))]
    seg = segment_ids.astype(F32)
    marks = jnp.stack(marks + [seg, seg], axis=1)
    segs = jnp.broadcast_to(seg[None], (8, tokens))
    params = jnp.pad(jnp.stack([decay_log, decay_bias]), ((0, 6), (0, 128 - heads)))
    gain = jnp.broadcast_to(head_gain[None], (8, dv))
    shared = (query_conv, key_conv, value_conv, marks, segs, params, gain)
    made = mixer_forward(heads, dk, dv, hidden, in_all, shared)
    pres, mixed, saved = made[:5], made[5], made[6:]
    mixed, grad_all = fence(mixed, grad_all)

    wide_inputs = inputs.astype(F32)

    half = tokens // 2
    first, last = slice(0, half), slice(half, tokens)

    cut_a = cut_cols(wide_dot(mixed[first], out_all), place, size)
    cut_b = cut_cols(wide_dot(after(mixed[last], cut_a), out_all), place, size)
    got_a = send_cols(cut_a[1], size)
    got_a, cut_b = fence(got_a, cut_b)

    got_b = send_cols(cut_b[1], size)
    residual_a = wide_inputs[first] + add_cols(cut_a[0], got_a)
    grad_sides = order_features(grad_all, rows)
    got_b, residual_a, grad_sides = fence(got_b, residual_a, grad_sides)

    all_a = hops(residual_a.astype(BF), size)
    residual_b = wide_inputs[last] + add_cols(cut_b[0], got_b)
    all_a, residual_b = fence(all_a, residual_b)

    def feed_forward(pieces, grad_rows):
        residual_all = lay_cols(pieces, place, size).astype(F32)
        scale = lax.rsqrt(jnp.mean(residual_all * residual_all, axis=1, keepdims=True) + 1e-05)
        (second,) = fence((residual_all * scale * second_gains).astype(BF))
        both = contract_features(second, mlp_all)
        gate_value, up_value = both[:, :hidden_units], both[:, hidden_units:]
        gate_sig = jax.nn.sigmoid(gate_value)
        gate_act = gate_value * gate_sig
        product = (gate_act * up_value).astype(BF)
        grad_product = contract_features(grad_rows, down_all)
        grad_both = jnp.concatenate(
            [grad_product * up_value * (gate_sig * (1.0 + gate_value * (1.0 - gate_sig))), grad_product * gate_act],
            axis=1,
        ).astype(BF)
        part = wide_dot(grad_both, mlp_all)
        inner = jnp.sum(part * second_gains * residual_all, axis=1)
        return scale, second, product, grad_both, inner, cut_cols(part, place, size)

    all_b = hops(residual_b.astype(BF), size)
    ready_a = feed_forward(all_a, grad_all[first])
    all_b, ready_a = fence(all_b, ready_a)

    scale_a, second_a, product_a, grad_both_a, inner_a, cut_a = ready_a
    got_a, inners_a = send_cols(cut_a[1], size), hops(inner_a, size)
    ready_b = feed_forward(all_b, grad_all[last])
    got_a, inners_a, ready_b = fence(got_a, inners_a, ready_b)

    def back_residual(at, residual, scale, inner, grad_second):
        return (
            cotangent[at].astype(F32)
            + scale * second_gain * grad_second
            - residual * (scale * scale * scale * inner[:, None] / model)
        )

    scale_b, second_b, product_b, grad_both_b, inner_b, cut_b = ready_b
    got_b, inners_b = send_cols(cut_b[1], size), hops(inner_b, size)
    grad_second_a = add_cols(cut_a[0], got_a)
    back_a = back_residual(first, residual_a, scale_a, sum(inners_a), grad_second_a)
    second = jnp.concatenate([second_a, second_b], axis=0)
    grad_both = jnp.concatenate([grad_both_a, grad_both_b], axis=0)
    product = jnp.concatenate([product_a, product_b], axis=0)
    mlp_part = contract_tokens(second, grad_both).astype(BF)
    mlp_grad = lax.psum_scatter(mlp_part, "row", scatter_dimension=0, tiled=True)
    away_down = away_part(grad_sides, product, rows)
    got_b, inners_b, back_a, mlp_part, away_down = fence(got_b, inners_b, back_a, mlp_part, away_down)

    pieces_a = hops(back_a.astype(BF), size)
    grad_second_b = add_cols(cut_b[0], got_b)
    back_b = back_residual(last, residual_b, scale_b, sum(inners_b), grad_second_b)
    near_down, given_down = near_part(grad_sides, product, away_down, rows)
    pieces_a, back_b, given_down = fence(pieces_a, back_b, given_down)

    pieces_b = hops(back_b.astype(BF), size)
    held_down = hold(near_down, given_down, rows)
    result_cut = cut_cols(wide_dot(product, down_all), place, size)
    back_rows_a = lay_cols(pieces_a, place, size)
    pieces_b, held_down, result_cut, back_rows_a = fence(pieces_b, held_down, result_cut, back_rows_a)

    residual = jnp.concatenate([residual_a, residual_b], axis=0)
    scale = jnp.concatenate([scale_a, scale_b], axis=0)
    grad_residual = jnp.concatenate([back_a, back_b], axis=0)
    second_gain_part = jnp.sum(
        jnp.concatenate([grad_second_a, grad_second_b], axis=0) * residual * scale, axis=0
    )
    back_rows = jnp.concatenate([back_rows_a, lay_cols(pieces_b, place, size)], axis=0)
    grad_mixed = contract_features(back_rows, out_all)
    x_down, y_down = send_chips(held_down, rows)
    out_part = contract_tokens(mixed, back_rows).astype(BF)
    out_part, mlp_grad = fence(out_part, mlp_grad)
    out_grad = lax.psum_scatter(out_part, "row", scatter_dimension=1, tiled=True)
    grad_mixed, result_cut = after((grad_mixed, result_cut), out_part)
    result_got = send_cols(result_cut[1], size)
    lows = mixer_backward(heads, dk, dv, pres, shared, grad_mixed, saved, 0, heads)
    lows, x_down, y_down, result_got = fence(lows, x_down, y_down, result_got)
    *lows, low_small, query_taps, key_taps, value_taps, params_part, gain_part = lows
    low = jnp.concatenate(per_half(lows, [dk, dk, dv, dv]) + [low_small], axis=1)
    down_late = last_step(held_down, x_down, y_down, rows)

    in_part = contract_tokens(hidden, low).astype(BF)
    in_grad = lax.psum_scatter(in_part, "row", scatter_dimension=0, tiled=True)
    hidden_part = contract_features(after(low, in_part), in_all)
    inner = jnp.sum(hidden_part * first_gains * wide_all, axis=1)
    hidden_cut = cut_cols(hidden_part, place, size)
    first_gain_part = jnp.sum(hidden_part * wide_all * first_scale, axis=0)
    notes = [
        jnp.concatenate(
            [inner, lax.dynamic_slice(first_gain_part, ((place + step) % size * width,), (width,)), gain_part[0]]
        )
        for step in range(size)
    ]
    notes, hidden_cut, down_late = fence(notes, hidden_cut, down_late)

    noted = sum([notes[0]] + send_cols(notes[1:], size))
    hidden_got = send_cols(hidden_cut[1], size)
    first_inner, gains = noted[:tokens, None], noted[tokens:]
    sums = [query_taps, key_taps, value_taps, params_part[0:2, :heads], second_gain_part, gains]
    query_taps, key_taps, value_taps, params_grad, second_gain_grad, gains = lax.psum(sums, "row")
    norm_gain_grad, gain_grad = gains[:width], gains[width:]
    result = add_cols(residual + result_cut[0], result_got)
    down_grad = finish(*down_late).T
    mlp_grad = mlp_grad.astype(F32)
    out_grad = out_grad.astype(F32)
    hidden_got, noted, down_grad, mlp_grad, out_grad, query_taps, result = fence(
        hidden_got, noted, down_grad, mlp_grad, out_grad, query_taps, result
    )

    grad_hidden = add_cols(hidden_cut[0], hidden_got)
    grad_inputs = (
        grad_residual
        + first_scale * norm_gain * grad_hidden
        - wide_inputs * (first_scale * first_scale * first_scale * first_inner / model)
    )
    in_grad, result, grad_inputs = fence(in_grad, result, grad_inputs)

    def head_columns(start, stop):
        return jnp.concatenate(
            [in_grad[:, half * span + each * start : half * span + each * stop] for half in (0, 1)], axis=1
        ).astype(F32)

    return (
        result,
        grad_inputs,
        norm_gain_grad,
        head_columns(0, dk),
        head_columns(dk, 2 * dk),
        head_columns(2 * dk, 2 * dk + dv),
        head_columns(2 * dk + dv, wide),
        in_grad[:, 2 * span : 2 * span + heads].astype(F32),
        in_grad[:, 2 * span + heads : 2 * span + 2 * heads].astype(F32),
        query_taps,
        key_taps,
        value_taps,
        params_grad[0],
        params_grad[1],
        gain_grad,
        out_grad,
        second_gain_grad,
        mlp_grad[:, :hidden_units],
        mlp_grad[:, hidden_units:],
        down_grad,
    )


ROW_COL = P("row", "col")
COL_ROW = P("col", "row")
PLACED = (
    ROW_COL, P("row"), P("col"),
    ROW_COL, ROW_COL, ROW_COL, ROW_COL, ROW_COL, ROW_COL,
    P(None, "col"), P(None, "col"), P(None, "col"),
    P("col"), P("col"), P(),
    COL_ROW, P("col"), ROW_COL, ROW_COL, COL_ROW, ROW_COL,
)
MADE = (
    ROW_COL, ROW_COL, P("col"),
    ROW_COL, ROW_COL, ROW_COL, ROW_COL, ROW_COL, ROW_COL,
    P(None, "col"), P(None, "col"), P(None, "col"),
    P("col"), P("col"), P(),
    COL_ROW, P("col"), ROW_COL, ROW_COL, COL_ROW,
)


def solution(mesh):
    return jax.shard_map(per_device, mesh=mesh, in_specs=PLACED, out_specs=MADE, check_vma=False)
```

```python
import functools
import jax
import jax.numpy as jnp
from jax import lax
from jax.experimental import pallas as pl
from jax.experimental.pallas import tpu as pltpu
from jax.sharding import PartitionSpec as P

BF = jnp.bfloat16
F32 = jnp.float32
BLOCK = 128
COST = pl.CostEstimate(flops=20_000_000_000, bytes_accessed=20_000_000, transcendentals=4_000_000)
VMEM = 56 * 1024 * 1024


def dot(left, right, lc=1, rc=0):
    return lax.dot_general(left, right, (((lc,), (rc,)), ((), ())), preferred_element_type=F32)


def split(x):
    high = x.astype(BF)
    return high, (x - high.astype(F32)).astype(BF)


def dot3(left, right, lc=1, rc=0):
    return (
        dot(left[0], right[0], lc, rc) + dot(left[0], right[1], lc, rc) + dot(left[1], right[0], lc, rc)
    )


def dotx(left, right, lc=1, rc=0):
    first = right.astype(BF)
    rest = right - first.astype(F32)
    second = rest.astype(BF)
    third = (rest - second.astype(F32)).astype(BF)
    return dot(left, first, lc, rc) + dot(left, second, lc, rc) + dot(left, third, lc, rc)


def sigmoid(x):
    return 0.5 + 0.5 * jnp.tanh(0.5 * x)


def lane_pick(block, lane):
    index = lax.broadcasted_iota(jnp.int32, block.shape, 1)
    return jnp.sum(jnp.where(index == lane, block, 0.0), axis=1, keepdims=True)


def row_pick(block, row):
    index = lax.broadcasted_iota(jnp.int32, block.shape, 0)
    return jnp.sum(jnp.where(index == row, block, 0.0), axis=0, keepdims=True)


def softplus(x):
    return jnp.maximum(x, 0.0) + jnp.log1p(jnp.exp(-jnp.abs(x)))


def conv_act(x, taps, marks):
    total = x * taps[3:4]
    for shift in (1, 2, 3):
        total = total + (marks[:, shift - 1 : shift] * pltpu.roll(x, shift, 0)) * taps[3 - shift : 4 - shift]
    gate = sigmoid(total)
    return total, gate


def grids():
    rows = lax.broadcasted_iota(jnp.int32, (BLOCK, BLOCK), 0)
    cols = lax.broadcasted_iota(jnp.int32, (BLOCK, BLOCK), 1)
    return rows, cols


def decays(small, params, head, heads):
    rate = jnp.exp(params[0:1])
    log_decay = -rate * softplus(small + params[1:2])
    beta = sigmoid(lane_pick(small, heads + head))
    return log_decay, beta


def block_decay(log_decay, head, rows, cols, seg_col, seg_row, last_seg):
    lower = (rows >= cols).astype(BF)
    running = dotx(lower, log_decay)
    column = lane_pick(running, head)
    line = row_pick(running.T, head)
    same = (seg_col == seg_row) & (rows >= cols)
    decay = jnp.where(same, jnp.exp(jnp.minimum(column - line, 0.0)), 0.0)
    carried = None
    if last_seg is not None:
        carried = jnp.where(seg_col == last_seg, jnp.exp(column), 0.0)
    return decay, carried


def unit_inverses(lowers, rows, cols):
    identity = (rows == cols).astype(F32)
    base = 16
    same = (rows // base) == (cols // base)
    nears = [jnp.where(same, -lower, 0.0) for lower in lowers]
    powers = [split(near) for near in nears]
    totals = [identity + near for near in nears]
    width = 2
    while width < base:
        powers = [split(dot3(power, power)) for power in powers]
        totals = [total + dot3(split(total), power) for total, power in zip(totals, powers)]
        width *= 2
    while base < BLOCK:
        pair_at = (rows // (2 * base) == cols // (2 * base)) & (rows // base != cols // base)
        offs = [split(jnp.where(pair_at, lower, 0.0)) for lower in lowers]
        parts = [split(total) for total in totals]
        middles = [split(dot3(off, part)) for off, part in zip(offs, parts)]
        totals = [total - dot3(part, middle) for total, part, middle in zip(totals, parts, middles)]
        base *= 2
    return totals


def head_inputs(pres, taps_refs, marks, dk, dv):
    heads = []
    for at in range(pres[0].shape[1] // dk):
        keyed, valued = slice(at * dk, (at + 1) * dk), slice(at * dv, (at + 1) * dv)
        spans = (keyed, keyed, valued)
        x = jnp.concatenate([pre[:, span] for pre, span in zip(pres, spans)], axis=1)
        taps = jnp.concatenate([ref[:, span] for ref, span in zip(taps_refs, spans)], axis=1)
        total, gate = conv_act(x, taps, marks)
        act = total * gate
        query_act, key_act, values = act[:, :dk], act[:, dk : 2 * dk], act[:, 2 * dk :]
        query_scale = lax.rsqrt(jnp.sum(query_act * query_act, axis=1, keepdims=True) + 1e-06)
        key_scale = lax.rsqrt(jnp.sum(key_act * key_act, axis=1, keepdims=True) + 1e-06)
        heads.append((x, taps, total, gate, query_act, key_act, values, query_scale, key_scale))
    return heads


def forward_kernel(heads, dk, dv, hidden_ref, query_weight, key_weight, value_weight, gate_weight, small_weight,
                   query_taps, key_taps, value_taps, marks_ref, segs_ref, params_ref, gain_ref,
                   query_ref, key_ref, value_ref, gate_ref, small_ref,
                   mixed_ref, out_ref, fresh_ref, mats_ref, states_ref):
    each = heads // 2
    hidden = hidden_ref[...]

    @pl.when(pl.program_id(0) == 0)
    def _():
        small_ref[...] = dot(hidden, small_weight[...])

    query_ref[...] = dot(hidden, query_weight[...])
    key_ref[...] = dot(hidden, key_weight[...])
    value_ref[...] = dot(hidden, value_weight[...])
    gate_ref[...] = dot(hidden, gate_weight[...])
    marks = marks_ref[...]
    small, params = small_ref[...], params_ref[...]
    tokens = hidden.shape[0]
    rows, cols = grids()
    blocks = tokens // BLOCK
    cuts = [slice(index * BLOCK, (index + 1) * BLOCK) for index in range(blocks)]
    own = []
    for at, parts in enumerate(
        head_inputs([query_ref[...], key_ref[...], value_ref[...]], (query_taps, key_taps, value_taps), marks, dk, dv)
    ):
        _, _, _, _, query_act, key_act, values, query_scale, key_scale = parts
        head = pl.program_id(0) * each + at
        queries = query_act * (query_scale * dk ** -0.5)
        keys = key_act * key_scale
        log_decay, beta = decays(small, params, head, heads)
        key_parts = [split(keys[cut]) for cut in cuts]
        query_parts = [split(queries[cut]) for cut in cuts]
        decay_pairs = [
            block_decay(
                log_decay[cut], head, rows, cols, marks[cut, 6:7], segs_ref[0:1, cut],
                marks[index * BLOCK - 1 : index * BLOCK, 6:7] if index else None,
            )
            for index, cut in enumerate(cuts)
        ]
        inners = [
            jnp.where(rows > cols, dot3(key, key, 1, 1) * two[0], 0.0) for key, two in zip(key_parts, decay_pairs)
        ]
        scores = [dot3(query, key, 1, 1) * two[0] for query, key, two in zip(query_parts, key_parts, decay_pairs)]
        own.append((keys, values, beta, key_parts, query_parts, decay_pairs, inners, scores))
    lowers = [head[2][cut] * inner for head in own for cut, inner in zip(cuts, head[6])]
    inverses = unit_inverses(lowers, rows, cols)
    states = [None] * each
    for index, cut in enumerate(cuts):
        for at, (keys, values, beta, key_parts, query_parts, decay_pairs, inners, scores) in enumerate(own):
            decay, carried = decay_pairs[index]
            score, inverse = scores[index], inverses[at * blocks + index]
            value, strength = values[cut], beta[cut]
            valued = slice(at * dv, (at + 1) * dv)
            mats_ref[cut, (3 * at) * BLOCK : (3 * at + 1) * BLOCK] = inners[index]
            mats_ref[cut, (3 * at + 1) * BLOCK : (3 * at + 2) * BLOCK] = score
            mats_ref[cut, (3 * at + 2) * BLOCK : (3 * at + 3) * BLOCK] = inverse
            if index:
                state_parts = split(states[at])
                source = strength * (value - carried * dot3(key_parts[index], state_parts))
            else:
                source = strength * value
            fresh = dot3(split(inverse), split(source))
            fresh_parts = split(fresh)
            output = dot3(split(score), fresh_parts)
            if index:
                output = output + carried * dot3(query_parts[index], state_parts)
            if index + 1 < blocks:
                grown = dot3(split(keys[cut] * lane_pick_row(decay)), fresh_parts, 0, 0)
                states[at] = grown if index == 0 else carried[BLOCK - 1 : BLOCK] * states[at] + grown
                states_ref[index * dk : (index + 1) * dk, valued] = states[at]
            fresh_ref[cut, valued] = fresh
            out_ref[cut, valued] = output
            scale = lax.rsqrt(jnp.mean(output * output, axis=1, keepdims=True) + 1e-05)
            gate_pre = gate_ref[cut, valued]
            mixed_ref[cut, valued] = (output * scale * gain_ref[0:1] * (gate_pre * sigmoid(gate_pre))).astype(BF)


def lane_pick_row(decay):
    return decay.T[:, BLOCK - 1 : BLOCK]


def in_turn(steps):
    while steps:
        steps = [step for step in steps if next(step, steps) is not steps]


def backward_kernel(heads, dk, dv, query_ref, key_ref, value_ref, gate_ref, small_ref, query_taps, key_taps, value_taps,
                    marks_ref, segs_ref, params_ref, gain_ref, grad_ref, out_ref, fresh_ref, mats_ref, states_ref,
                    low_query_ref, low_key_ref, low_value_ref, low_gate_ref, low_small_ref,
                    query_taps_grad, key_taps_grad, value_taps_grad, params_grad_ref, gain_grad_ref):
    each = heads // 2

    @pl.when(pl.program_id(0) == 0)
    def _():
        low_small_ref[...] = jnp.zeros_like(low_small_ref)
        params_grad_ref[...] = jnp.zeros_like(params_grad_ref)
        gain_grad_ref[...] = jnp.zeros_like(gain_grad_ref)

    marks = marks_ref[...]
    small = small_ref[...]
    params = params_ref[...]
    inputs = head_inputs(
        [query_ref[...], key_ref[...], value_ref[...]], (query_taps, key_taps, value_taps), marks, dk, dv
    )
    tokens = small.shape[0]
    rows, cols = grids()
    gain = gain_ref[0:1]
    blocks = tokens // BLOCK
    upper = (rows <= cols).astype(BF)
    at_last = lax.broadcasted_iota(jnp.int32, (BLOCK, 1), 0) == BLOCK - 1
    own = []
    for at, (_, _, _, _, query_act, key_act, values, query_scale, key_scale) in enumerate(inputs):
        head = pl.program_id(0) * each + at
        own.append(
            (head, query_act * (query_scale * dk ** -0.5), key_act * key_scale, values)
            + decays(small, params, head, heads)
        )
    d_states = [None] * each
    d_query = [[None] * blocks for _ in range(each)]
    d_key = [[None] * blocks for _ in range(each)]
    d_value = [[None] * blocks for _ in range(each)]
    d_beta = [[None] * blocks for _ in range(each)]
    d_decay = [[None] * blocks for _ in range(each)]
    kept = {}
    gain_sums = []

    def before(index, at):
        head, queries, keys, values, log_decay, beta = own[at]
        cut = slice(index * BLOCK, (index + 1) * BLOCK)
        valued = slice(at * dv, (at + 1) * dv)
        grad = grad_ref[cut, valued]
        output = out_ref[cut, valued]
        gate_pre = gate_ref[cut, valued]
        gate_sig = sigmoid(gate_pre)
        gate_act = gate_pre * gate_sig
        scale = lax.rsqrt(jnp.mean(output * output, axis=1, keepdims=True) + 1e-05)
        normed = output * scale
        both = grad * normed
        gain_sums.append(jnp.sum(both * gate_act, axis=0, keepdims=True))
        low_gate_ref[cut, valued] = (both * gain * (gate_sig + gate_act * (1.0 - gate_sig))).astype(BF)
        pulled = grad * gate_act * gain
        d_out = scale * (pulled - normed * jnp.mean(pulled * normed, axis=1, keepdims=True))
        yield
        last_seg = marks[index * BLOCK - 1 : index * BLOCK, 6:7] if index else None
        decay, carried = block_decay(
            log_decay[cut], head, rows, cols, marks[cut, 6:7], segs_ref[0:1, cut], last_seg
        )
        yield
        score = mats_ref[cut, (3 * at + 1) * BLOCK : (3 * at + 2) * BLOCK]
        fresh_parts = split(fresh_ref[cut, valued])
        out_parts = split(d_out)
        d_fresh = dot3(split(score), out_parts, 0, 0)
        d_score = dot3(out_parts, fresh_parts, 1, 1)
        yield
        key, query = keys[cut], queries[cut]
        key_parts, query_parts = split(key), split(query)
        change = d_score * score
        d_scores = split(d_score * decay)
        dq = dot3(d_scores, key_parts)
        dk_ = dot3(d_scores, query_parts, 0, 0)
        yield
        state_parts, d_carried, from_query = None, None, None
        if index:
            state_parts = split(states_ref[(index - 1) * dk : index * dk, valued])
            out_back = dot3(out_parts, state_parts, 1, 1)
            from_query = dot3(query_parts, split(carried * d_out), 0, 0)
            d_carried = jnp.sum(query * out_back, axis=1, keepdims=True)
            dq = dq + carried * out_back
        d_query[at][index] = dq
        kept[index, at] = (decay, carried, fresh_parts, key_parts, d_fresh, change, dk_, state_parts, d_carried, from_query)

    def through(index, at):
        _, _, keys, _, _, beta = own[at]
        cut = slice(index * BLOCK, (index + 1) * BLOCK)
        decay, carried, _, key_parts, d_fresh, _, _, _, _, from_query = kept[index, at]
        inverse = mats_ref[cut, (3 * at + 2) * BLOCK : (3 * at + 3) * BLOCK]
        d_state, tail, state_grad_parts = d_states[at], None, None
        if d_state is not None:
            tail = lane_pick_row(decay)
            state_grad_parts = split(d_state)
            d_fresh = d_fresh + dot3(split(keys[cut] * tail), state_grad_parts)
        yield
        d_source = dot3(split(inverse), split(d_fresh), 0, 0)
        yield
        if index:
            new_state = from_query - dot3(key_parts, split((beta[cut] * carried) * d_source), 0, 0)
            d_states[at] = new_state if d_state is None else new_state + carried[BLOCK - 1 : BLOCK] * d_state
        kept[index, at] += (d_state, tail, state_grad_parts, d_source)

    def behind(index, at):
        _, _, keys, values, _, beta = own[at]
        cut = slice(index * BLOCK, (index + 1) * BLOCK)
        valued = slice(at * dv, (at + 1) * dv)
        (decay, carried, fresh_parts, key_parts, _, change, dk_, state_parts, d_carried, _,
         d_state, tail, state_grad_parts, d_source) = kept.pop((index, at))
        key, strength = keys[cut], beta[cut]
        inner = mats_ref[cut, (3 * at) * BLOCK : (3 * at + 1) * BLOCK]
        source_parts = split(d_source)
        d_lower = jnp.where(rows > cols, -dot3(source_parts, fresh_parts, 1, 1), 0.0)
        yield
        d_value[at][index] = strength * d_source
        d_strength = jnp.sum(d_source * values[cut], axis=1, keepdims=True) + jnp.sum(
            d_lower * inner, axis=1, keepdims=True
        )
        change = change + d_lower * (strength * inner)
        d_run = jnp.sum(change, axis=1, keepdims=True) - jnp.sum(change.T, axis=1, keepdims=True)
        d_inners = split(d_lower * (strength * decay))
        dk_ = dk_ + dot3(d_inners, key_parts) + dot3(d_inners, key_parts, 0, 0)
        yield
        last_extra = None
        if d_state is not None:
            moved = dot3(fresh_parts, state_grad_parts, 1, 1)
            dk_ = dk_ + tail * moved
            d_tail = jnp.sum(key * moved, axis=1, keepdims=True) * tail
            d_run = d_run - d_tail
            last_extra = jnp.sum(d_tail, axis=0, keepdims=True)
        yield
        if index:
            source_back = dot3(source_parts, state_parts, 1, 1)
            key_source = jnp.sum(key * source_back, axis=1, keepdims=True)
            d_strength = d_strength - carried * key_source
            dk_ = dk_ - (strength * carried) * source_back
            d_run = d_run + (d_carried - strength * key_source) * carried
            if d_state is not None:
                state = states_ref[(index - 1) * dk : index * dk, valued]
                kept_sum = jnp.sum(jnp.sum(state * d_state, axis=1, keepdims=True), axis=0, keepdims=True)
                last_extra = last_extra + kept_sum * carried[BLOCK - 1 : BLOCK]
        if last_extra is not None:
            d_run = d_run + jnp.where(at_last, last_extra, 0.0)
        yield
        d_decay[at][index] = dotx(upper, jnp.broadcast_to(d_run, (BLOCK, BLOCK)))[:, 0:1]
        d_key[at][index], d_beta[at][index] = dk_, d_strength

    backwards = list(reversed(range(blocks)))
    for index in backwards:
        in_turn([before(index, at) for at in range(each)])
    for index in backwards:
        in_turn([through(index, at) for at in range(each)])
    for index in backwards:
        in_turn([behind(index, at) for at in range(each)])
    d_gain = sum(gain_sums)

    lane = lax.broadcasted_iota(jnp.int32, small.shape, 1)
    rate = jnp.exp(params[0:1])
    for at, (x, taps, total, gate, query_act, key_act, values, query_scale, key_scale) in enumerate(inputs):
        head, _, _, _, log_decay, beta = own[at]
        keyed, valued = slice(at * dk, (at + 1) * dk), slice(at * dv, (at + 1) * dv)
        dq = jnp.concatenate(d_query[at], axis=0) * dk ** -0.5
        dk_ = jnp.concatenate(d_key[at], axis=0)
        dv_ = jnp.concatenate(d_value[at], axis=0)
        query_pull = jnp.sum(dq * query_act, axis=1, keepdims=True)
        key_pull = jnp.sum(dk_ * key_act, axis=1, keepdims=True)
        d_query_act = query_scale * (dq - query_act * (query_scale * query_scale * query_pull))
        d_key_act = key_scale * (dk_ - key_act * (key_scale * key_scale * key_pull))
        d_act = jnp.concatenate([d_query_act, d_key_act, dv_], axis=1)
        d_total = d_act * (gate * (1.0 + total * (1.0 - gate)))
        d_pre = d_total * taps[3:4]
        tap_sums = [None, None, None, jnp.sum(d_total * x, axis=0, keepdims=True)]
        for shift in (1, 2, 3):
            moved = marks[:, 2 + shift : 3 + shift] * pltpu.roll(d_total, tokens - shift, 0)
            d_pre = d_pre + moved * taps[3 - shift : 4 - shift]
            tap_sums[3 - shift] = jnp.sum(moved * x, axis=0, keepdims=True)
        d_pre = d_pre.astype(BF)
        low_query_ref[:, keyed] = d_pre[:, :dk]
        low_key_ref[:, keyed] = d_pre[:, dk : 2 * dk]
        low_value_ref[:, valued] = d_pre[:, 2 * dk :]
        for tap in range(4):
            query_taps_grad[tap : tap + 1, keyed] = tap_sums[tap][:, :dk]
            key_taps_grad[tap : tap + 1, keyed] = tap_sums[tap][:, dk : 2 * dk]
            value_taps_grad[tap : tap + 1, valued] = tap_sums[tap][:, 2 * dk :]
        d_log = jnp.concatenate(d_decay[at], axis=0)
        d_str = jnp.concatenate(d_beta[at], axis=0)
        d_decay_pre = jnp.where(lane == head, d_log * (-rate) * sigmoid(small + params[1:2]), 0.0)
        d_beta_pre = jnp.where(lane == heads + head, d_str * beta * (1.0 - beta), 0.0)
        low_small_ref[...] += (d_decay_pre + d_beta_pre).astype(BF)
        params_grad_ref[0:1, :] += jnp.sum(jnp.where(lane == head, d_log * log_decay, 0.0), axis=0, keepdims=True)
        params_grad_ref[1:2, :] += jnp.sum(d_decay_pre, axis=0, keepdims=True)
    gain_grad_ref[0:1, :] += d_gain


def whole(h):
    return (0, 0)


def own_half(g):
    return (0, g)


def shared_specs(tokens, heads, dk, dv):
    each = heads // 2
    return [
        pl.BlockSpec((4, each * dk), own_half),
        pl.BlockSpec((4, each * dk), own_half),
        pl.BlockSpec((4, each * dv), own_half),
        pl.BlockSpec((tokens, 8), whole),
        pl.BlockSpec((8, tokens), whole),
        pl.BlockSpec((8, 128), whole),
        pl.BlockSpec((8, dv), whole),
    ]


def pre_specs(tokens, heads, dk, dv):
    each = heads // 2
    return [
        pl.BlockSpec((tokens, each * dk), own_half),
        pl.BlockSpec((tokens, each * dk), own_half),
        pl.BlockSpec((tokens, each * dv), own_half),
        pl.BlockSpec((tokens, each * dv), own_half),
        pl.BlockSpec((tokens, 128), whole),
    ]


def saved_specs(tokens, heads, dk, dv):
    each = heads // 2
    blocks = tokens // BLOCK
    return [
        pl.BlockSpec((tokens, each * dv), own_half),
        pl.BlockSpec((tokens, each * dv), own_half),
        pl.BlockSpec((tokens, each * 3 * BLOCK), own_half),
        pl.BlockSpec(((blocks - 1) * dk, each * dv), own_half),
    ]


def mixer_forward(heads, dk, dv, hidden, weight, shared):
    tokens, model = hidden.shape
    blocks = tokens // BLOCK
    each = heads // 2
    wide = 2 * dk + 2 * dv

    def columns(before):
        return lambda g: (0, before + g)

    return pl.pallas_call(
        functools.partial(forward_kernel, heads, dk, dv),
        grid=(2,),
        in_specs=[
            pl.BlockSpec((tokens, model), whole),
            pl.BlockSpec((model, each * dk), columns(0)),
            pl.BlockSpec((model, each * dk), columns(2)),
            pl.BlockSpec((model, each * dv), columns(4 * dk // dv)),
            pl.BlockSpec((model, each * dv), columns(4 * dk // dv + 2)),
            pl.BlockSpec((model, 128), lambda g: (0, heads * wide // 128)),
        ]
        + shared_specs(tokens, heads, dk, dv),
        out_specs=pre_specs(tokens, heads, dk, dv)
        + [pl.BlockSpec((tokens, each * dv), own_half)]
        + saved_specs(tokens, heads, dk, dv),
        out_shape=[
            jax.ShapeDtypeStruct((tokens, heads * dk), F32),
            jax.ShapeDtypeStruct((tokens, heads * dk), F32),
            jax.ShapeDtypeStruct((tokens, heads * dv), F32),
            jax.ShapeDtypeStruct((tokens, heads * dv), F32),
            jax.ShapeDtypeStruct((tokens, 128), F32),
            jax.ShapeDtypeStruct((tokens, heads * dv), BF),
            jax.ShapeDtypeStruct((tokens, heads * dv), F32),
            jax.ShapeDtypeStruct((tokens, heads * dv), F32),
            jax.ShapeDtypeStruct((tokens, heads * 3 * BLOCK), F32),
            jax.ShapeDtypeStruct(((blocks - 1) * dk, heads * dv), F32),
        ],
        compiler_params=pltpu.CompilerParams(vmem_limit_bytes=VMEM),
        cost_estimate=COST,
        name="mixer_forward",
    )(hidden, weight, weight, weight, weight, weight, *shared)


def mixer_backward(heads, dk, dv, pres, shared, grad, saved):
    tokens = grad.shape[0]
    each = heads // 2
    return pl.pallas_call(
        functools.partial(backward_kernel, heads, dk, dv),
        grid=(2,),
        in_specs=pre_specs(tokens, heads, dk, dv)
        + shared_specs(tokens, heads, dk, dv)
        + [pl.BlockSpec((tokens, each * dv), own_half)]
        + saved_specs(tokens, heads, dk, dv),
        out_specs=[
            pl.BlockSpec((tokens, each * dk), own_half),
            pl.BlockSpec((tokens, each * dk), own_half),
            pl.BlockSpec((tokens, each * dv), own_half),
            pl.BlockSpec((tokens, each * dv), own_half),
            pl.BlockSpec((tokens, 128), whole),
            pl.BlockSpec((4, each * dk), own_half),
            pl.BlockSpec((4, each * dk), own_half),
            pl.BlockSpec((4, each * dv), own_half),
            pl.BlockSpec((8, 128), whole),
            pl.BlockSpec((8, dv), whole),
        ],
        out_shape=[
            jax.ShapeDtypeStruct((tokens, heads * dk), BF),
            jax.ShapeDtypeStruct((tokens, heads * dk), BF),
            jax.ShapeDtypeStruct((tokens, heads * dv), BF),
            jax.ShapeDtypeStruct((tokens, heads * dv), BF),
            jax.ShapeDtypeStruct((tokens, 128), BF),
            jax.ShapeDtypeStruct((4, heads * dk), F32),
            jax.ShapeDtypeStruct((4, heads * dk), F32),
            jax.ShapeDtypeStruct((4, heads * dv), F32),
            jax.ShapeDtypeStruct((8, 128), F32),
            jax.ShapeDtypeStruct((8, dv), F32),
        ],
        compiler_params=pltpu.CompilerParams(vmem_limit_bytes=VMEM),
        cost_estimate=COST,
        name="mixer_backward",
    )(*pres, *shared, grad, *saved)


def wide_dot(left, right):
    return jnp.dot(left, right, preferred_element_type=F32)


def contract_tokens(left, right):
    return dot(left, right, 0, 0)


def contract_features(left, right):
    return dot(left, right, 1, 1)


def after(values, *first):
    return lax.optimization_barrier((values, first))[0]


def fence(*values):
    return lax.optimization_barrier(values)


def hop(values, step, size):
    return lax.ppermute(values, "col", [(at, at ^ step) for at in range(size)])


def hops(values, size):
    return [values] + [hop(values, step, size) for step in range(1, size)]


def lay(pieces, spots, width):
    whole = jnp.zeros((pieces[0].shape[0], len(pieces) * width), pieces[0].dtype)
    for piece, spot in zip(pieces, spots):
        whole = lax.dynamic_update_slice(whole, piece, (0, spot * width))
    return whole


def gather_cols(values, place, size):
    return lay_cols(hops(values, size), place, size)


def lay_cols(pieces, place, size):
    return lay(pieces, [place ^ step for step in range(size)], pieces[0].shape[1])


def send_cols(pieces, size):
    return [hop(piece, step + 1, size) for step, piece in enumerate(pieces)]


def add_cols(own, received):
    for piece in received:
        own = own + piece.astype(F32)
    return own


def cut_cols(partial_sum, place, size):
    rows, width = partial_sum.shape[0], partial_sum.shape[1] // size
    own = lax.dynamic_slice(partial_sum, (0, place * width), (rows, width))
    return own, [
        lax.dynamic_slice(partial_sum, (0, (place ^ step) * width), (rows, width)).astype(BF)
        for step in range(1, size)
    ]


def pair(values, mask, rows):
    return lax.ppermute(values, "row", [(at, at ^ mask) for at in range(rows)])


def chips(rows):
    return rows == 8


def order_features(values, rows):
    if not chips(rows):
        return [values]
    here = lax.axis_index("row")
    depth = values.shape[1] // rows
    return [
        jnp.concatenate(
            [
                lax.dynamic_slice(values, (0, (here ^ chip ^ core) * depth), (values.shape[0], depth))
                for chip in (0, 2, 4, 6)
            ],
            axis=1,
        )
        for core in (0, 1)
    ]


def away_part(left, right, rows):
    return contract_tokens(left[1], right).astype(BF) if chips(rows) else None


def near_part(left, right, away, rows):
    if not chips(rows):
        return contract_tokens(left[0], right).astype(BF), None
    return (left[0], right), pair(away, 1, rows)


def hold(near, given, rows):
    return near if given is None else (contract_tokens(*near) + given.astype(F32)).astype(BF)


def send_chips(held, rows):
    if not chips(rows):
        return None, None
    depth = held.shape[0] // 4
    half = depth // 2
    own, x, y, far = (held[at * depth : (at + 1) * depth] for at in range(4))
    from_x = pair(jnp.concatenate([far[:half], x[:half]], axis=0), 2, rows)
    from_y = pair(jnp.concatenate([far[half:], y[half:]], axis=0), 4, rows)
    return from_x, from_y


def last_step(held, from_x, from_y, rows):
    if from_x is None:
        return lax.psum_scatter(held, "row", scatter_dimension=0, tiled=True), None, None, None
    depth = held.shape[0] // 4
    half = depth // 2
    own, x, y, far = (held[at * depth : (at + 1) * depth] for at in range(4))
    last_x = pair((x[half:].astype(F32) + from_y[:half].astype(F32)).astype(BF), 2, rows)
    last_y = pair((y[:half].astype(F32) + from_x[:half].astype(F32)).astype(BF), 4, rows)
    mine = own.astype(F32) + jnp.concatenate([from_x[half:], from_y[half:]], axis=0).astype(F32)
    return mine, last_x, last_y, rows


def finish(mine, last_x, last_y, rows):
    if last_x is None:
        return mine.astype(F32)
    return mine + jnp.concatenate([last_y, last_x], axis=0).astype(F32)


def per_device(
    inputs,
    segment_ids,
    norm_gain,
    query_weight,
    key_weight,
    value_weight,
    gate_weight,
    decay_weight,
    beta_weight,
    query_conv,
    key_conv,
    value_conv,
    decay_log,
    decay_bias,
    head_gain,
    out_weight,
    second_gain,
    hidden_gate,
    hidden_up,
    hidden_down,
    cotangent,
):
    tokens, width = inputs.shape
    size = lax.axis_size("col")
    rows = lax.axis_size("row")
    place = lax.axis_index("col")
    model = size * width
    heads = decay_weight.shape[1]
    dk = query_weight.shape[1] // heads
    dv = value_weight.shape[1] // heads
    depth = query_weight.shape[0]
    hidden_units = hidden_gate.shape[1]
    wide = 2 * dk + 2 * dv

    in_weight = jnp.concatenate(
        [
            query_weight, key_weight, value_weight, gate_weight, decay_weight, beta_weight,
            jnp.zeros((depth, 128 - 2 * heads), BF),
        ],
        axis=1,
    )
    inputs_all = gather_cols(inputs, place, size)
    gains_all = gather_cols(jnp.stack([norm_gain, second_gain]), place, size)
    in_all = lax.all_gather(in_weight, "row", axis=0, tiled=True)
    out_all = lax.all_gather(out_weight, "row", axis=1, tiled=True)
    hidden_gate, hidden_up, hidden_down = after((hidden_gate, hidden_up, hidden_down), in_weight)
    stacked = jnp.concatenate([hidden_gate.T, hidden_up.T, hidden_down], axis=0)
    stacked = lax.all_gather(stacked, "row", axis=1, tiled=True)
    mlp_all, down_all = stacked[: 2 * hidden_units], stacked[2 * hidden_units :]
    first_gains, second_gains = gains_all[0:1], gains_all[1:2]

    wide_all = inputs_all.astype(F32)
    first_scale = lax.rsqrt(jnp.mean(wide_all * wide_all, axis=1, keepdims=True) + 1e-05)
    hidden, in_all, cotangent_late = fence((wide_all * first_scale * first_gains).astype(BF), in_all, cotangent)
    grad_all = gather_cols(cotangent_late, place, size)

    times = jnp.arange(tokens)
    marks = [
        jnp.where((times >= shift) & (jnp.roll(segment_ids, shift) == segment_ids), 1.0, 0.0) for shift in (1, 2, 3)
    ]
    marks = marks + [jnp.roll(mark, -shift) for mark, shift in zip(marks, (1, 2, 3))]
    seg = segment_ids.astype(F32)
    marks = jnp.stack(marks + [seg, seg], axis=1)
    segs = jnp.broadcast_to(seg[None], (8, tokens))
    params = jnp.pad(jnp.stack([decay_log, decay_bias]), ((0, 6), (0, 128 - heads)))
    gain = jnp.broadcast_to(head_gain[None], (8, dv))
    shared = (query_conv, key_conv, value_conv, marks, segs, params, gain)
    made = mixer_forward(heads, dk, dv, hidden, in_all, shared)
    pres, mixed, saved = made[:5], made[5], made[6:]
    mixed, grad_all = fence(mixed, grad_all)

    wide_inputs = inputs.astype(F32)

    half = tokens // 2
    first, last = slice(0, half), slice(half, tokens)

    cut_a = cut_cols(wide_dot(mixed[first], out_all), place, size)
    cut_b = cut_cols(wide_dot(after(mixed[last], cut_a), out_all), place, size)
    got_a = send_cols(cut_a[1], size)
    got_a, cut_b = fence(got_a, cut_b)

    got_b = send_cols(cut_b[1], size)
    residual_a = wide_inputs[first] + add_cols(cut_a[0], got_a)
    grad_sides = order_features(grad_all, rows)
    got_b, residual_a, grad_sides = fence(got_b, residual_a, grad_sides)

    all_a = hops(residual_a.astype(BF), size)
    residual_b = wide_inputs[last] + add_cols(cut_b[0], got_b)
    all_a, residual_b = fence(all_a, residual_b)

    def feed_forward(pieces, grad_rows):
        residual_all = lay_cols(pieces, place, size).astype(F32)
        scale = lax.rsqrt(jnp.mean(residual_all * residual_all, axis=1, keepdims=True) + 1e-05)
        (second,) = fence((residual_all * scale * second_gains).astype(BF))
        both = contract_features(second, mlp_all)
        gate_value, up_value = both[:, :hidden_units], both[:, hidden_units:]
        gate_sig = jax.nn.sigmoid(gate_value)
        gate_act = gate_value * gate_sig
        product = (gate_act * up_value).astype(BF)
        grad_product = contract_features(grad_rows, down_all)
        grad_both = jnp.concatenate(
            [grad_product * up_value * (gate_sig * (1.0 + gate_value * (1.0 - gate_sig))), grad_product * gate_act],
            axis=1,
        ).astype(BF)
        part = wide_dot(grad_both, mlp_all)
        inner = jnp.sum(part * second_gains * residual_all, axis=1)
        return scale, second, product, grad_both, inner, cut_cols(part, place, size)

    all_b = hops(residual_b.astype(BF), size)
    ready_a = feed_forward(all_a, grad_all[first])
    all_b, ready_a = fence(all_b, ready_a)

    scale_a, second_a, product_a, grad_both_a, inner_a, cut_a = ready_a
    got_a, inners_a = send_cols(cut_a[1], size), hops(inner_a, size)
    ready_b = feed_forward(all_b, grad_all[last])
    got_a, inners_a, ready_b = fence(got_a, inners_a, ready_b)

    def back_residual(at, residual, scale, inner, grad_second):
        return (
            cotangent[at].astype(F32)
            + scale * second_gain * grad_second
            - residual * (scale * scale * scale * inner[:, None] / model)
        )

    scale_b, second_b, product_b, grad_both_b, inner_b, cut_b = ready_b
    got_b, inners_b = send_cols(cut_b[1], size), hops(inner_b, size)
    grad_second_a = add_cols(cut_a[0], got_a)
    back_a = back_residual(first, residual_a, scale_a, sum(inners_a), grad_second_a)
    second = jnp.concatenate([second_a, second_b], axis=0)
    grad_both = jnp.concatenate([grad_both_a, grad_both_b], axis=0)
    product = jnp.concatenate([product_a, product_b], axis=0)
    mlp_part = contract_tokens(second, grad_both).astype(BF)
    mlp_grad = lax.psum_scatter(mlp_part, "row", scatter_dimension=0, tiled=True)
    away_down = away_part(grad_sides, product, rows)
    got_b, inners_b, back_a, mlp_part, away_down = fence(got_b, inners_b, back_a, mlp_part, away_down)

    pieces_a = hops(back_a.astype(BF), size)
    grad_second_b = add_cols(cut_b[0], got_b)
    back_b = back_residual(last, residual_b, scale_b, sum(inners_b), grad_second_b)
    near_down, given_down = near_part(grad_sides, product, away_down, rows)
    pieces_a, back_b, given_down, product = fence(pieces_a, back_b, given_down, product)

    pieces_b = hops(back_b.astype(BF), size)
    held_down = hold(near_down, given_down, rows)
    result_cut = cut_cols(wide_dot(product, down_all), place, size)
    back_rows_a = lay_cols(pieces_a, place, size)
    pieces_b, held_down, result_cut, back_rows_a = fence(pieces_b, held_down, result_cut, back_rows_a)

    residual = jnp.concatenate([residual_a, residual_b], axis=0)
    scale = jnp.concatenate([scale_a, scale_b], axis=0)
    grad_residual = jnp.concatenate([back_a, back_b], axis=0)
    second_gain_part = jnp.sum(
        jnp.concatenate([grad_second_a, grad_second_b], axis=0) * residual * scale, axis=0
    )
    back_rows = jnp.concatenate([back_rows_a, lay_cols(pieces_b, place, size)], axis=0)
    grad_mixed = contract_features(back_rows, out_all)
    x_down, y_down = send_chips(held_down, rows)
    out_part = contract_tokens(mixed, back_rows).astype(BF)
    out_part, mlp_grad, grad_mixed, result_cut = fence(out_part, mlp_grad, grad_mixed, result_cut)
    out_grad = lax.psum_scatter(out_part, "row", scatter_dimension=1, tiled=True)
    result_got = send_cols(result_cut[1], size)
    lows = mixer_backward(heads, dk, dv, pres, shared, grad_mixed, saved)
    lows, x_down, y_down, result_got = fence(lows, x_down, y_down, result_got)
    *lows, low_small, query_taps, key_taps, value_taps, params_part, gain_part = lows
    low = jnp.concatenate(lows + [low_small], axis=1)
    down_late = last_step(held_down, x_down, y_down, rows)

    in_part = contract_tokens(hidden, low).astype(BF)
    in_grad = lax.psum_scatter(in_part, "row", scatter_dimension=0, tiled=True)
    hidden_part = contract_features(after(low, in_part), in_all)
    inner = jnp.sum(hidden_part * first_gains * wide_all, axis=1)
    hidden_cut = cut_cols(hidden_part, place, size)
    first_gain_part = jnp.sum(hidden_part * wide_all * first_scale, axis=0)
    notes = [
        jnp.concatenate(
            [inner, lax.dynamic_slice(first_gain_part, ((place ^ step) * width,), (width,)), gain_part[0]]
        )
        for step in range(size)
    ]
    notes, hidden_cut, down_late = fence(notes, hidden_cut, down_late)

    noted = sum([notes[0]] + send_cols(notes[1:], size))
    hidden_got = send_cols(hidden_cut[1], size)
    first_inner, gains = noted[:tokens, None], noted[tokens:]
    sums = [query_taps, key_taps, value_taps, params_part[0:2, :heads], second_gain_part, gains]
    query_taps, key_taps, value_taps, params_grad, second_gain_grad, gains = lax.psum(sums, "row")
    norm_gain_grad, gain_grad = gains[:width], gains[width:]
    result = add_cols(residual + result_cut[0], result_got)
    down_grad = finish(*down_late).T
    mlp_grad = mlp_grad.astype(F32)
    out_grad = out_grad.astype(F32)
    hidden_got, noted, down_grad, mlp_grad, out_grad, query_taps, result = fence(
        hidden_got, noted, down_grad, mlp_grad, out_grad, query_taps, result
    )

    grad_hidden = add_cols(hidden_cut[0], hidden_got)
    grad_inputs = (
        grad_residual
        + first_scale * norm_gain * grad_hidden
        - wide_inputs * (first_scale * first_scale * first_scale * first_inner / model)
    )
    in_grad, result, grad_inputs = fence(in_grad, result, grad_inputs)

    def head_columns(start, stop):
        return in_grad[:, heads * start : heads * stop].astype(F32)

    return (
        result,
        grad_inputs,
        norm_gain_grad,
        head_columns(0, dk),
        head_columns(dk, 2 * dk),
        head_columns(2 * dk, 2 * dk + dv),
        head_columns(2 * dk + dv, wide),
        in_grad[:, heads * wide : heads * wide + heads].astype(F32),
        in_grad[:, heads * wide + heads : heads * wide + 2 * heads].astype(F32),
        query_taps,
        key_taps,
        value_taps,
        params_grad[0],
        params_grad[1],
        gain_grad,
        out_grad,
        second_gain_grad,
        mlp_grad[:, :hidden_units],
        mlp_grad[:, hidden_units:],
        down_grad,
    )


ROW_COL = P("row", "col")
COL_ROW = P("col", "row")
PLACED = (
    ROW_COL, P("row"), P("col"),
    ROW_COL, ROW_COL, ROW_COL, ROW_COL, ROW_COL, ROW_COL,
    P(None, "col"), P(None, "col"), P(None, "col"),
    P("col"), P("col"), P(),
    COL_ROW, P("col"), ROW_COL, ROW_COL, COL_ROW, ROW_COL,
)
MADE = (
    ROW_COL, ROW_COL, P("col"),
    ROW_COL, ROW_COL, ROW_COL, ROW_COL, ROW_COL, ROW_COL,
    P(None, "col"), P(None, "col"), P(None, "col"),
    P("col"), P("col"), P(),
    COL_ROW, P("col"), ROW_COL, ROW_COL, COL_ROW,
)


def solution(mesh):
    return jax.shard_map(per_device, mesh=mesh, in_specs=PLACED, out_specs=MADE, check_vma=False)
```

```python
import functools
import jax
import jax.numpy as jnp
from jax import lax
from jax.experimental import pallas as pl
from jax.experimental.pallas import tpu as pltpu
from jax.sharding import PartitionSpec as P

BF = jnp.bfloat16
F32 = jnp.float32
BLOCK = 128
COST = pl.CostEstimate(flops=20_000_000_000, bytes_accessed=20_000_000, transcendentals=4_000_000)
VMEM = 56 * 1024 * 1024


def dot(left, right, lc=1, rc=0):
    return lax.dot_general(left, right, (((lc,), (rc,)), ((), ())), preferred_element_type=F32)


def split(x):
    high = x.astype(BF)
    return high, (x - high.astype(F32)).astype(BF)


def dot3(left, right, lc=1, rc=0):
    return (
        dot(left[0], right[0], lc, rc) + dot(left[0], right[1], lc, rc) + dot(left[1], right[0], lc, rc)
    )


def dotx(left, right, lc=1, rc=0):
    first = right.astype(BF)
    rest = right - first.astype(F32)
    second = rest.astype(BF)
    third = (rest - second.astype(F32)).astype(BF)
    return dot(left, first, lc, rc) + dot(left, second, lc, rc) + dot(left, third, lc, rc)


def sigmoid(x):
    return 0.5 + 0.5 * jnp.tanh(0.5 * x)


def lane_pick(block, lane):
    index = lax.broadcasted_iota(jnp.int32, block.shape, 1)
    return jnp.sum(jnp.where(index == lane, block, 0.0), axis=1, keepdims=True)


def row_pick(block, row):
    index = lax.broadcasted_iota(jnp.int32, block.shape, 0)
    return jnp.sum(jnp.where(index == row, block, 0.0), axis=0, keepdims=True)


def softplus(x):
    return jnp.maximum(x, 0.0) + jnp.log1p(jnp.exp(-jnp.abs(x)))


def conv_act(x, taps, marks):
    total = x * taps[3:4]
    for shift in (1, 2, 3):
        total = total + (marks[:, shift - 1 : shift] * pltpu.roll(x, shift, 0)) * taps[3 - shift : 4 - shift]
    gate = sigmoid(total)
    return total, gate


def grids():
    rows = lax.broadcasted_iota(jnp.int32, (BLOCK, BLOCK), 0)
    cols = lax.broadcasted_iota(jnp.int32, (BLOCK, BLOCK), 1)
    return rows, cols


def decays(small, params, head, heads):
    rate = jnp.exp(params[0:1])
    log_decay = -rate * softplus(small + params[1:2])
    beta = sigmoid(lane_pick(small, heads + head))
    return log_decay, beta


def block_decay(log_decay, head, rows, cols, seg_col, seg_row, last_seg):
    lower = (rows >= cols).astype(BF)
    running = dotx(lower, log_decay)
    column = lane_pick(running, head)
    line = row_pick(running.T, head)
    same = (seg_col == seg_row) & (rows >= cols)
    decay = jnp.where(same, jnp.exp(jnp.minimum(column - line, 0.0)), 0.0)
    carried = None
    if last_seg is not None:
        carried = jnp.where(seg_col == last_seg, jnp.exp(column), 0.0)
    return decay, carried


def unit_inverses(lowers, rows, cols):
    identity = (rows == cols).astype(F32)
    base = 16
    same = (rows // base) == (cols // base)
    nears = [jnp.where(same, -lower, 0.0) for lower in lowers]
    powers = [split(near) for near in nears]
    totals = [identity + near for near in nears]
    width = 2
    while width < base:
        powers = [split(dot3(power, power)) for power in powers]
        totals = [total + dot3(split(total), power) for total, power in zip(totals, powers)]
        width *= 2
    while base < BLOCK:
        pair_at = (rows // (2 * base) == cols // (2 * base)) & (rows // base != cols // base)
        offs = [split(jnp.where(pair_at, lower, 0.0)) for lower in lowers]
        parts = [split(total) for total in totals]
        middles = [split(dot3(off, part)) for off, part in zip(offs, parts)]
        totals = [total - dot3(part, middle) for total, part, middle in zip(totals, parts, middles)]
        base *= 2
    return totals


def head_inputs(pres, taps_refs, marks, dk, dv):
    heads = []
    for at in range(pres[0].shape[1] // dk):
        keyed, valued = slice(at * dk, (at + 1) * dk), slice(at * dv, (at + 1) * dv)
        spans = (keyed, keyed, valued)
        x = jnp.concatenate([pre[:, span] for pre, span in zip(pres, spans)], axis=1)
        taps = jnp.concatenate([ref[:, span] for ref, span in zip(taps_refs, spans)], axis=1)
        total, gate = conv_act(x, taps, marks)
        act = total * gate
        query_act, key_act, values = act[:, :dk], act[:, dk : 2 * dk], act[:, 2 * dk :]
        query_scale = lax.rsqrt(jnp.sum(query_act * query_act, axis=1, keepdims=True) + 1e-06)
        key_scale = lax.rsqrt(jnp.sum(key_act * key_act, axis=1, keepdims=True) + 1e-06)
        heads.append((x, taps, total, gate, query_act, key_act, values, query_scale, key_scale))
    return heads


def forward_kernel(heads, dk, dv, hidden_ref, query_weight, key_weight, value_weight, gate_weight, small_weight,
                   query_taps, key_taps, value_taps, marks_ref, segs_ref, params_ref, gain_ref,
                   query_ref, key_ref, value_ref, gate_ref, small_ref,
                   mixed_ref, out_ref, fresh_ref, mats_ref, states_ref):
    each = heads // 2
    hidden = hidden_ref[...]

    @pl.when(pl.program_id(0) == 0)
    def _():
        small_ref[...] = dot(hidden, small_weight[...])

    query_ref[...] = dot(hidden, query_weight[...])
    key_ref[...] = dot(hidden, key_weight[...])
    value_ref[...] = dot(hidden, value_weight[...])
    gate_ref[...] = dot(hidden, gate_weight[...])
    marks = marks_ref[...]
    small, params = small_ref[...], params_ref[...]
    tokens = hidden.shape[0]
    rows, cols = grids()
    blocks = tokens // BLOCK
    cuts = [slice(index * BLOCK, (index + 1) * BLOCK) for index in range(blocks)]
    own = []
    for at, parts in enumerate(
        head_inputs([query_ref[...], key_ref[...], value_ref[...]], (query_taps, key_taps, value_taps), marks, dk, dv)
    ):
        _, _, _, _, query_act, key_act, values, query_scale, key_scale = parts
        head = pl.program_id(0) * each + at
        queries = query_act * (query_scale * dk ** -0.5)
        keys = key_act * key_scale
        log_decay, beta = decays(small, params, head, heads)
        key_parts = [split(keys[cut]) for cut in cuts]
        query_parts = [split(queries[cut]) for cut in cuts]
        decay_pairs = [
            block_decay(
                log_decay[cut], head, rows, cols, marks[cut, 6:7], segs_ref[0:1, cut],
                marks[index * BLOCK - 1 : index * BLOCK, 6:7] if index else None,
            )
            for index, cut in enumerate(cuts)
        ]
        inners = [
            jnp.where(rows > cols, dot3(key, key, 1, 1) * two[0], 0.0) for key, two in zip(key_parts, decay_pairs)
        ]
        scores = [dot3(query, key, 1, 1) * two[0] for query, key, two in zip(query_parts, key_parts, decay_pairs)]
        own.append((keys, values, beta, key_parts, query_parts, decay_pairs, inners, scores))
    lowers = [head[2][cut] * inner for head in own for cut, inner in zip(cuts, head[6])]
    inverses = unit_inverses(lowers, rows, cols)
    states = [None] * each
    for index, cut in enumerate(cuts):
        for at, (keys, values, beta, key_parts, query_parts, decay_pairs, inners, scores) in enumerate(own):
            decay, carried = decay_pairs[index]
            score, inverse = scores[index], inverses[at * blocks + index]
            value, strength = values[cut], beta[cut]
            valued = slice(at * dv, (at + 1) * dv)
            mats_ref[cut, (3 * at) * BLOCK : (3 * at + 1) * BLOCK] = inners[index]
            mats_ref[cut, (3 * at + 1) * BLOCK : (3 * at + 2) * BLOCK] = score
            mats_ref[cut, (3 * at + 2) * BLOCK : (3 * at + 3) * BLOCK] = inverse
            if index:
                state_parts = split(states[at])
                source = strength * (value - carried * dot3(key_parts[index], state_parts))
            else:
                source = strength * value
            fresh = dot3(split(inverse), split(source))
            fresh_parts = split(fresh)
            output = dot3(split(score), fresh_parts)
            if index:
                output = output + carried * dot3(query_parts[index], state_parts)
            if index + 1 < blocks:
                grown = dot3(split(keys[cut] * lane_pick_row(decay)), fresh_parts, 0, 0)
                states[at] = grown if index == 0 else carried[BLOCK - 1 : BLOCK] * states[at] + grown
                states_ref[index * dk : (index + 1) * dk, valued] = states[at]
            fresh_ref[cut, valued] = fresh
            out_ref[cut, valued] = output
            scale = lax.rsqrt(jnp.mean(output * output, axis=1, keepdims=True) + 1e-05)
            gate_pre = gate_ref[cut, valued]
            mixed_ref[cut, valued] = (output * scale * gain_ref[0:1] * (gate_pre * sigmoid(gate_pre))).astype(BF)


def lane_pick_row(decay):
    return decay.T[:, BLOCK - 1 : BLOCK]


def in_turn(steps):
    while steps:
        steps = [step for step in steps if next(step, steps) is not steps]


def backward_kernel(heads, dk, dv, query_ref, key_ref, value_ref, gate_ref, small_ref, query_taps, key_taps, value_taps,
                    marks_ref, segs_ref, params_ref, gain_ref, grad_ref, out_ref, fresh_ref, mats_ref, states_ref,
                    low_query_ref, low_key_ref, low_value_ref, low_gate_ref, low_small_ref,
                    query_taps_grad, key_taps_grad, value_taps_grad, params_grad_ref, gain_grad_ref):
    each = heads // 2

    @pl.when(pl.program_id(0) == 0)
    def _():
        low_small_ref[...] = jnp.zeros_like(low_small_ref)
        params_grad_ref[...] = jnp.zeros_like(params_grad_ref)
        gain_grad_ref[...] = jnp.zeros_like(gain_grad_ref)

    marks = marks_ref[...]
    small = small_ref[...]
    params = params_ref[...]
    inputs = head_inputs(
        [query_ref[...], key_ref[...], value_ref[...]], (query_taps, key_taps, value_taps), marks, dk, dv
    )
    tokens = small.shape[0]
    rows, cols = grids()
    gain = gain_ref[0:1]
    blocks = tokens // BLOCK
    upper = (rows <= cols).astype(BF)
    at_last = lax.broadcasted_iota(jnp.int32, (BLOCK, 1), 0) == BLOCK - 1
    own = []
    for at, (_, _, _, _, query_act, key_act, values, query_scale, key_scale) in enumerate(inputs):
        head = pl.program_id(0) * each + at
        own.append(
            (head, query_act * (query_scale * dk ** -0.5), key_act * key_scale, values)
            + decays(small, params, head, heads)
        )
    d_states = [None] * each
    d_query = [[None] * blocks for _ in range(each)]
    d_key = [[None] * blocks for _ in range(each)]
    d_value = [[None] * blocks for _ in range(each)]
    d_beta = [[None] * blocks for _ in range(each)]
    d_decay = [[None] * blocks for _ in range(each)]
    kept = {}
    gain_sums = []

    def before(index, at):
        head, queries, keys, values, log_decay, beta = own[at]
        cut = slice(index * BLOCK, (index + 1) * BLOCK)
        valued = slice(at * dv, (at + 1) * dv)
        grad = grad_ref[cut, valued]
        output = out_ref[cut, valued]
        gate_pre = gate_ref[cut, valued]
        gate_sig = sigmoid(gate_pre)
        gate_act = gate_pre * gate_sig
        scale = lax.rsqrt(jnp.mean(output * output, axis=1, keepdims=True) + 1e-05)
        normed = output * scale
        both = grad * normed
        gain_sums.append(jnp.sum(both * gate_act, axis=0, keepdims=True))
        low_gate_ref[cut, valued] = (both * gain * (gate_sig + gate_act * (1.0 - gate_sig))).astype(BF)
        pulled = grad * gate_act * gain
        d_out = scale * (pulled - normed * jnp.mean(pulled * normed, axis=1, keepdims=True))
        yield
        last_seg = marks[index * BLOCK - 1 : index * BLOCK, 6:7] if index else None
        decay, carried = block_decay(
            log_decay[cut], head, rows, cols, marks[cut, 6:7], segs_ref[0:1, cut], last_seg
        )
        yield
        score = mats_ref[cut, (3 * at + 1) * BLOCK : (3 * at + 2) * BLOCK]
        fresh_parts = split(fresh_ref[cut, valued])
        out_parts = split(d_out)
        d_fresh = dot3(split(score), out_parts, 0, 0)
        d_score = dot3(out_parts, fresh_parts, 1, 1)
        yield
        key, query = keys[cut], queries[cut]
        key_parts, query_parts = split(key), split(query)
        change = d_score * score
        d_scores = split(d_score * decay)
        dq = dot3(d_scores, key_parts)
        dk_ = dot3(d_scores, query_parts, 0, 0)
        yield
        state_parts, d_carried, from_query = None, None, None
        if index:
            state_parts = split(states_ref[(index - 1) * dk : index * dk, valued])
            out_back = dot3(out_parts, state_parts, 1, 1)
            from_query = dot3(query_parts, split(carried * d_out), 0, 0)
            d_carried = jnp.sum(query * out_back, axis=1, keepdims=True)
            dq = dq + carried * out_back
        d_query[at][index] = dq
        kept[index, at] = (decay, carried, fresh_parts, key_parts, d_fresh, change, dk_, state_parts, d_carried, from_query)

    def through(index, at):
        _, _, keys, _, _, beta = own[at]
        cut = slice(index * BLOCK, (index + 1) * BLOCK)
        decay, carried, _, key_parts, d_fresh, _, _, _, _, from_query = kept[index, at]
        inverse = mats_ref[cut, (3 * at + 2) * BLOCK : (3 * at + 3) * BLOCK]
        d_state, tail, state_grad_parts = d_states[at], None, None
        if d_state is not None:
            tail = lane_pick_row(decay)
            state_grad_parts = split(d_state)
            d_fresh = d_fresh + dot3(split(keys[cut] * tail), state_grad_parts)
        yield
        d_source = dot3(split(inverse), split(d_fresh), 0, 0)
        yield
        if index:
            new_state = from_query - dot3(key_parts, split((beta[cut] * carried) * d_source), 0, 0)
            d_states[at] = new_state if d_state is None else new_state + carried[BLOCK - 1 : BLOCK] * d_state
        kept[index, at] += (d_state, tail, state_grad_parts, d_source)

    def behind(index, at):
        _, _, keys, values, _, beta = own[at]
        cut = slice(index * BLOCK, (index + 1) * BLOCK)
        valued = slice(at * dv, (at + 1) * dv)
        (decay, carried, fresh_parts, key_parts, _, change, dk_, state_parts, d_carried, _,
         d_state, tail, state_grad_parts, d_source) = kept.pop((index, at))
        key, strength = keys[cut], beta[cut]
        inner = mats_ref[cut, (3 * at) * BLOCK : (3 * at + 1) * BLOCK]
        source_parts = split(d_source)
        d_lower = jnp.where(rows > cols, -dot3(source_parts, fresh_parts, 1, 1), 0.0)
        yield
        d_value[at][index] = strength * d_source
        d_strength = jnp.sum(d_source * values[cut], axis=1, keepdims=True) + jnp.sum(
            d_lower * inner, axis=1, keepdims=True
        )
        change = change + d_lower * (strength * inner)
        d_run = jnp.sum(change, axis=1, keepdims=True) - jnp.sum(change.T, axis=1, keepdims=True)
        d_inners = split(d_lower * (strength * decay))
        dk_ = dk_ + dot3(d_inners, key_parts) + dot3(d_inners, key_parts, 0, 0)
        yield
        last_extra = None
        if d_state is not None:
            moved = dot3(fresh_parts, state_grad_parts, 1, 1)
            dk_ = dk_ + tail * moved
            d_tail = jnp.sum(key * moved, axis=1, keepdims=True) * tail
            d_run = d_run - d_tail
            last_extra = jnp.sum(d_tail, axis=0, keepdims=True)
        yield
        if index:
            source_back = dot3(source_parts, state_parts, 1, 1)
            key_source = jnp.sum(key * source_back, axis=1, keepdims=True)
            d_strength = d_strength - carried * key_source
            dk_ = dk_ - (strength * carried) * source_back
            d_run = d_run + (d_carried - strength * key_source) * carried
            if d_state is not None:
                state = states_ref[(index - 1) * dk : index * dk, valued]
                kept_sum = jnp.sum(jnp.sum(state * d_state, axis=1, keepdims=True), axis=0, keepdims=True)
                last_extra = last_extra + kept_sum * carried[BLOCK - 1 : BLOCK]
        if last_extra is not None:
            d_run = d_run + jnp.where(at_last, last_extra, 0.0)
        yield
        d_decay[at][index] = dotx(upper, jnp.broadcast_to(d_run, (BLOCK, BLOCK)))[:, 0:1]
        d_key[at][index], d_beta[at][index] = dk_, d_strength

    backwards = list(reversed(range(blocks)))
    for index in backwards:
        in_turn([before(index, at) for at in range(each)])
    for index in backwards:
        in_turn([through(index, at) for at in range(each)])
    for index in backwards:
        in_turn([behind(index, at) for at in range(each)])
    d_gain = sum(gain_sums)

    lane = lax.broadcasted_iota(jnp.int32, small.shape, 1)
    rate = jnp.exp(params[0:1])
    for at, (x, taps, total, gate, query_act, key_act, values, query_scale, key_scale) in enumerate(inputs):
        head, _, _, _, log_decay, beta = own[at]
        keyed, valued = slice(at * dk, (at + 1) * dk), slice(at * dv, (at + 1) * dv)
        dq = jnp.concatenate(d_query[at], axis=0) * dk ** -0.5
        dk_ = jnp.concatenate(d_key[at], axis=0)
        dv_ = jnp.concatenate(d_value[at], axis=0)
        query_pull = jnp.sum(dq * query_act, axis=1, keepdims=True)
        key_pull = jnp.sum(dk_ * key_act, axis=1, keepdims=True)
        d_query_act = query_scale * (dq - query_act * (query_scale * query_scale * query_pull))
        d_key_act = key_scale * (dk_ - key_act * (key_scale * key_scale * key_pull))
        d_act = jnp.concatenate([d_query_act, d_key_act, dv_], axis=1)
        d_total = d_act * (gate * (1.0 + total * (1.0 - gate)))
        d_pre = d_total * taps[3:4]
        tap_sums = [None, None, None, jnp.sum(d_total * x, axis=0, keepdims=True)]
        for shift in (1, 2, 3):
            moved = marks[:, 2 + shift : 3 + shift] * pltpu.roll(d_total, tokens - shift, 0)
            d_pre = d_pre + moved * taps[3 - shift : 4 - shift]
            tap_sums[3 - shift] = jnp.sum(moved * x, axis=0, keepdims=True)
        d_pre = d_pre.astype(BF)
        low_query_ref[:, keyed] = d_pre[:, :dk]
        low_key_ref[:, keyed] = d_pre[:, dk : 2 * dk]
        low_value_ref[:, valued] = d_pre[:, 2 * dk :]
        for tap in range(4):
            query_taps_grad[tap : tap + 1, keyed] = tap_sums[tap][:, :dk]
            key_taps_grad[tap : tap + 1, keyed] = tap_sums[tap][:, dk : 2 * dk]
            value_taps_grad[tap : tap + 1, valued] = tap_sums[tap][:, 2 * dk :]
        d_log = jnp.concatenate(d_decay[at], axis=0)
        d_str = jnp.concatenate(d_beta[at], axis=0)
        d_decay_pre = jnp.where(lane == head, d_log * (-rate) * sigmoid(small + params[1:2]), 0.0)
        d_beta_pre = jnp.where(lane == heads + head, d_str * beta * (1.0 - beta), 0.0)
        low_small_ref[...] += (d_decay_pre + d_beta_pre).astype(BF)
        params_grad_ref[0:1, :] += jnp.sum(jnp.where(lane == head, d_log * log_decay, 0.0), axis=0, keepdims=True)
        params_grad_ref[1:2, :] += jnp.sum(d_decay_pre, axis=0, keepdims=True)
    gain_grad_ref[0:1, :] += d_gain


def whole(h):
    return (0, 0)


def own_half(g):
    return (0, g)


def shared_specs(tokens, heads, dk, dv):
    each = heads // 2
    return [
        pl.BlockSpec((4, each * dk), own_half),
        pl.BlockSpec((4, each * dk), own_half),
        pl.BlockSpec((4, each * dv), own_half),
        pl.BlockSpec((tokens, 8), whole),
        pl.BlockSpec((8, tokens), whole),
        pl.BlockSpec((8, 128), whole),
        pl.BlockSpec((8, dv), whole),
    ]


def pre_specs(tokens, heads, dk, dv):
    each = heads // 2
    return [
        pl.BlockSpec((tokens, each * dk), own_half),
        pl.BlockSpec((tokens, each * dk), own_half),
        pl.BlockSpec((tokens, each * dv), own_half),
        pl.BlockSpec((tokens, each * dv), own_half),
        pl.BlockSpec((tokens, 128), whole),
    ]


def saved_specs(tokens, heads, dk, dv):
    each = heads // 2
    blocks = tokens // BLOCK
    return [
        pl.BlockSpec((tokens, each * dv), own_half),
        pl.BlockSpec((tokens, each * dv), own_half),
        pl.BlockSpec((tokens, each * 3 * BLOCK), own_half),
        pl.BlockSpec(((blocks - 1) * dk, each * dv), own_half),
    ]


def mixer_forward(heads, dk, dv, hidden, weight, shared):
    tokens, model = hidden.shape
    blocks = tokens // BLOCK
    each = heads // 2
    wide = 2 * dk + 2 * dv

    def columns(before):
        return lambda g: (0, before + g)

    return pl.pallas_call(
        functools.partial(forward_kernel, heads, dk, dv),
        grid=(2,),
        in_specs=[
            pl.BlockSpec((tokens, model), whole),
            pl.BlockSpec((model, each * dk), columns(0)),
            pl.BlockSpec((model, each * dk), columns(2)),
            pl.BlockSpec((model, each * dv), columns(4 * dk // dv)),
            pl.BlockSpec((model, each * dv), columns(4 * dk // dv + 2)),
            pl.BlockSpec((model, 128), lambda g: (0, heads * wide // 128)),
        ]
        + shared_specs(tokens, heads, dk, dv),
        out_specs=pre_specs(tokens, heads, dk, dv)
        + [pl.BlockSpec((tokens, each * dv), own_half)]
        + saved_specs(tokens, heads, dk, dv),
        out_shape=[
            jax.ShapeDtypeStruct((tokens, heads * dk), F32),
            jax.ShapeDtypeStruct((tokens, heads * dk), F32),
            jax.ShapeDtypeStruct((tokens, heads * dv), F32),
            jax.ShapeDtypeStruct((tokens, heads * dv), F32),
            jax.ShapeDtypeStruct((tokens, 128), F32),
            jax.ShapeDtypeStruct((tokens, heads * dv), BF),
            jax.ShapeDtypeStruct((tokens, heads * dv), F32),
            jax.ShapeDtypeStruct((tokens, heads * dv), F32),
            jax.ShapeDtypeStruct((tokens, heads * 3 * BLOCK), F32),
            jax.ShapeDtypeStruct(((blocks - 1) * dk, heads * dv), F32),
        ],
        compiler_params=pltpu.CompilerParams(vmem_limit_bytes=VMEM),
        cost_estimate=COST,
        name="mixer_forward",
    )(hidden, weight, weight, weight, weight, weight, *shared)


def mixer_backward(heads, dk, dv, pres, shared, grad, saved):
    tokens = grad.shape[0]
    each = heads // 2
    return pl.pallas_call(
        functools.partial(backward_kernel, heads, dk, dv),
        grid=(2,),
        in_specs=pre_specs(tokens, heads, dk, dv)
        + shared_specs(tokens, heads, dk, dv)
        + [pl.BlockSpec((tokens, each * dv), own_half)]
        + saved_specs(tokens, heads, dk, dv),
        out_specs=[
            pl.BlockSpec((tokens, each * dk), own_half),
            pl.BlockSpec((tokens, each * dk), own_half),
            pl.BlockSpec((tokens, each * dv), own_half),
            pl.BlockSpec((tokens, each * dv), own_half),
            pl.BlockSpec((tokens, 128), whole),
            pl.BlockSpec((4, each * dk), own_half),
            pl.BlockSpec((4, each * dk), own_half),
            pl.BlockSpec((4, each * dv), own_half),
            pl.BlockSpec((8, 128), whole),
            pl.BlockSpec((8, dv), whole),
        ],
        out_shape=[
            jax.ShapeDtypeStruct((tokens, heads * dk), BF),
            jax.ShapeDtypeStruct((tokens, heads * dk), BF),
            jax.ShapeDtypeStruct((tokens, heads * dv), BF),
            jax.ShapeDtypeStruct((tokens, heads * dv), BF),
            jax.ShapeDtypeStruct((tokens, 128), BF),
            jax.ShapeDtypeStruct((4, heads * dk), F32),
            jax.ShapeDtypeStruct((4, heads * dk), F32),
            jax.ShapeDtypeStruct((4, heads * dv), F32),
            jax.ShapeDtypeStruct((8, 128), F32),
            jax.ShapeDtypeStruct((8, dv), F32),
        ],
        compiler_params=pltpu.CompilerParams(vmem_limit_bytes=VMEM),
        cost_estimate=COST,
        name="mixer_backward",
    )(*pres, *shared, grad, *saved)


def wide_dot(left, right):
    return jnp.dot(left, right, preferred_element_type=F32)


def contract_tokens(left, right):
    return dot(left, right, 0, 0)


def contract_features(left, right):
    return dot(left, right, 1, 1)


def after(values, *first):
    return lax.optimization_barrier((values, first))[0]


def fence(*values):
    return lax.optimization_barrier(values)


def hop(values, step, size):
    return lax.ppermute(values, "col", [(at, at ^ step) for at in range(size)])


def hops(values, size):
    return [values] + [hop(values, step, size) for step in range(1, size)]


def lay(pieces, spots, width):
    whole = jnp.zeros((pieces[0].shape[0], len(pieces) * width), pieces[0].dtype)
    for piece, spot in zip(pieces, spots):
        whole = lax.dynamic_update_slice(whole, piece, (0, spot * width))
    return whole


def gather_cols(values, place, size):
    return lay_cols(hops(values, size), place, size)


def lay_cols(pieces, place, size):
    return lay(pieces, [place ^ step for step in range(size)], pieces[0].shape[1])


def send_cols(pieces, size):
    return [hop(piece, step + 1, size) for step, piece in enumerate(pieces)]


def add_cols(own, received):
    for piece in received:
        own = own + piece.astype(F32)
    return own


def cut_cols(partial_sum, place, size):
    rows, width = partial_sum.shape[0], partial_sum.shape[1] // size
    own = lax.dynamic_slice(partial_sum, (0, place * width), (rows, width))
    return own, [
        lax.dynamic_slice(partial_sum, (0, (place ^ step) * width), (rows, width)).astype(BF)
        for step in range(1, size)
    ]


def pair(values, mask, rows):
    return lax.ppermute(values, "row", [(at, at ^ mask) for at in range(rows)])


def chips(rows):
    return rows == 8


def order_features(values, rows):
    if not chips(rows):
        return [values]
    here = lax.axis_index("row")
    depth = values.shape[1] // rows
    return [
        jnp.concatenate(
            [
                lax.dynamic_slice(values, (0, (here ^ chip ^ core) * depth), (values.shape[0], depth))
                for chip in (0, 2, 4, 6)
            ],
            axis=1,
        )
        for core in (0, 1)
    ]


def away_part(left, right, rows):
    return contract_tokens(left[1], right).astype(BF) if chips(rows) else None


def near_part(left, right, away, rows):
    if not chips(rows):
        return contract_tokens(left[0], right).astype(BF), None
    return (left[0], right), pair(away, 1, rows)


def hold(near, given, rows):
    return near if given is None else (contract_tokens(*near) + given.astype(F32)).astype(BF)


def send_chips(held, rows):
    if not chips(rows):
        return None, None
    depth = held.shape[0] // 4
    half = depth // 2
    own, x, y, far = (held[at * depth : (at + 1) * depth] for at in range(4))
    from_x = pair(jnp.concatenate([far[:half], x[:half]], axis=0), 2, rows)
    from_y = pair(jnp.concatenate([far[half:], y[half:]], axis=0), 4, rows)
    return from_x, from_y


def last_step(held, from_x, from_y, rows):
    if from_x is None:
        return lax.psum_scatter(held, "row", scatter_dimension=0, tiled=True), None, None, None
    depth = held.shape[0] // 4
    half = depth // 2
    own, x, y, far = (held[at * depth : (at + 1) * depth] for at in range(4))
    last_x = pair((x[half:].astype(F32) + from_y[:half].astype(F32)).astype(BF), 2, rows)
    last_y = pair((y[:half].astype(F32) + from_x[:half].astype(F32)).astype(BF), 4, rows)
    mine = own.astype(F32) + jnp.concatenate([from_x[half:], from_y[half:]], axis=0).astype(F32)
    return mine, last_x, last_y, rows


def finish(mine, last_x, last_y, rows):
    if last_x is None:
        return mine.astype(F32)
    return mine + jnp.concatenate([last_y, last_x], axis=0).astype(F32)


def per_device(
    inputs,
    segment_ids,
    norm_gain,
    query_weight,
    key_weight,
    value_weight,
    gate_weight,
    decay_weight,
    beta_weight,
    query_conv,
    key_conv,
    value_conv,
    decay_log,
    decay_bias,
    head_gain,
    out_weight,
    second_gain,
    hidden_gate,
    hidden_up,
    hidden_down,
    cotangent,
):
    tokens, width = inputs.shape
    size = lax.axis_size("col")
    rows = lax.axis_size("row")
    place = lax.axis_index("col")
    model = size * width
    heads = decay_weight.shape[1]
    dk = query_weight.shape[1] // heads
    dv = value_weight.shape[1] // heads
    depth = query_weight.shape[0]
    hidden_units = hidden_gate.shape[1]
    wide = 2 * dk + 2 * dv

    in_weight = jnp.concatenate(
        [
            query_weight, key_weight, value_weight, gate_weight, decay_weight, beta_weight,
            jnp.zeros((depth, 128 - 2 * heads), BF),
        ],
        axis=1,
    )
    inputs_all = gather_cols(inputs, place, size)
    gains_all = gather_cols(jnp.stack([norm_gain, second_gain]), place, size)
    in_all = lax.all_gather(in_weight, "row", axis=0, tiled=True)
    out_all = lax.all_gather(out_weight, "row", axis=1, tiled=True)
    hidden_gate, hidden_up, hidden_down = after((hidden_gate, hidden_up, hidden_down), in_weight)
    stacked = jnp.concatenate([hidden_gate.T, hidden_up.T, hidden_down], axis=0)
    stacked = lax.all_gather(stacked, "row", axis=1, tiled=True)
    mlp_all, down_all = stacked[: 2 * hidden_units], stacked[2 * hidden_units :]
    first_gains, second_gains = gains_all[0:1], gains_all[1:2]

    wide_all = inputs_all.astype(F32)
    first_scale = lax.rsqrt(jnp.mean(wide_all * wide_all, axis=1, keepdims=True) + 1e-05)
    hidden, in_all, cotangent_late = fence((wide_all * first_scale * first_gains).astype(BF), in_all, cotangent)
    grad_all = gather_cols(cotangent_late, place, size)

    times = jnp.arange(tokens)
    marks = [
        jnp.where((times >= shift) & (jnp.roll(segment_ids, shift) == segment_ids), 1.0, 0.0) for shift in (1, 2, 3)
    ]
    marks = marks + [jnp.roll(mark, -shift) for mark, shift in zip(marks, (1, 2, 3))]
    seg = segment_ids.astype(F32)
    marks = jnp.stack(marks + [seg, seg], axis=1)
    segs = jnp.broadcast_to(seg[None], (8, tokens))
    params = jnp.pad(jnp.stack([decay_log, decay_bias]), ((0, 6), (0, 128 - heads)))
    gain = jnp.broadcast_to(head_gain[None], (8, dv))
    shared = (query_conv, key_conv, value_conv, marks, segs, params, gain)
    made = mixer_forward(heads, dk, dv, hidden, in_all, shared)
    pres, mixed, saved = made[:5], made[5], made[6:]
    mixed, grad_all = fence(mixed, grad_all)

    wide_inputs = inputs.astype(F32)

    half = tokens // 2
    first, last = slice(0, half), slice(half, tokens)

    cut_a = cut_cols(wide_dot(mixed[first], out_all), place, size)
    cut_b = cut_cols(wide_dot(after(mixed[last], cut_a), out_all), place, size)
    got_a = send_cols(cut_a[1], size)
    got_a, cut_b = fence(got_a, cut_b)

    got_b = send_cols(cut_b[1], size)
    residual_a = wide_inputs[first] + add_cols(cut_a[0], got_a)
    grad_sides = order_features(grad_all, rows)
    got_b, residual_a, grad_sides = fence(got_b, residual_a, grad_sides)

    all_a = hops(residual_a.astype(BF), size)
    residual_b = wide_inputs[last] + add_cols(cut_b[0], got_b)
    all_a, residual_b = fence(all_a, residual_b)

    def feed_forward(pieces, grad_rows):
        residual_all = lay_cols(pieces, place, size).astype(F32)
        scale = lax.rsqrt(jnp.mean(residual_all * residual_all, axis=1, keepdims=True) + 1e-05)
        (second,) = fence((residual_all * scale * second_gains).astype(BF))
        both = contract_features(second, mlp_all)
        gate_value, up_value = both[:, :hidden_units], both[:, hidden_units:]
        gate_sig = jax.nn.sigmoid(gate_value)
        gate_act = gate_value * gate_sig
        product = (gate_act * up_value).astype(BF)
        grad_product = contract_features(grad_rows, down_all)
        grad_both = jnp.concatenate(
            [grad_product * up_value * (gate_sig * (1.0 + gate_value * (1.0 - gate_sig))), grad_product * gate_act],
            axis=1,
        ).astype(BF)
        part = wide_dot(grad_both, mlp_all)
        inner = jnp.sum(part * second_gains * residual_all, axis=1)
        return scale, second, product, grad_both, inner, cut_cols(part, place, size)

    all_b = hops(residual_b.astype(BF), size)
    ready_a = feed_forward(all_a, grad_all[first])
    all_b, ready_a = fence(all_b, ready_a)

    scale_a, second_a, product_a, grad_both_a, inner_a, cut_a = ready_a
    got_a, inners_a = send_cols(cut_a[1], size), hops(inner_a, size)
    ready_b = feed_forward(all_b, grad_all[last])
    got_a, inners_a, ready_b = fence(got_a, inners_a, ready_b)

    def back_residual(at, residual, scale, inner, grad_second):
        return (
            cotangent[at].astype(F32)
            + scale * second_gain * grad_second
            - residual * (scale * scale * scale * inner[:, None] / model)
        )

    scale_b, second_b, product_b, grad_both_b, inner_b, cut_b = ready_b
    got_b, inners_b = send_cols(cut_b[1], size), hops(inner_b, size)
    grad_second_a = add_cols(cut_a[0], got_a)
    back_a = back_residual(first, residual_a, scale_a, sum(inners_a), grad_second_a)
    second = jnp.concatenate([second_a, second_b], axis=0)
    grad_both = jnp.concatenate([grad_both_a, grad_both_b], axis=0)
    product = jnp.concatenate([product_a, product_b], axis=0)
    mlp_part = contract_tokens(second, grad_both).astype(BF)
    mlp_grad = lax.psum_scatter(mlp_part, "row", scatter_dimension=0, tiled=True)
    away_down = away_part(grad_sides, product, rows)
    got_b, inners_b, back_a, mlp_part, away_down = fence(got_b, inners_b, back_a, mlp_part, away_down)

    pieces_a = hops(back_a.astype(BF), size)
    grad_second_b = add_cols(cut_b[0], got_b)
    back_b = back_residual(last, residual_b, scale_b, sum(inners_b), grad_second_b)
    near_down, given_down = near_part(grad_sides, product, away_down, rows)
    pieces_a, back_b, given_down, product = fence(pieces_a, back_b, given_down, product)

    pieces_b = hops(back_b.astype(BF), size)
    held_down = hold(near_down, given_down, rows)
    result_cut = cut_cols(wide_dot(product, down_all), place, size)
    back_rows_a = lay_cols(pieces_a, place, size)
    pieces_b, held_down, result_cut, back_rows_a = fence(pieces_b, held_down, result_cut, back_rows_a)

    residual = jnp.concatenate([residual_a, residual_b], axis=0)
    scale = jnp.concatenate([scale_a, scale_b], axis=0)
    grad_residual = jnp.concatenate([back_a, back_b], axis=0)
    second_gain_part = jnp.sum(
        jnp.concatenate([grad_second_a, grad_second_b], axis=0) * residual * scale, axis=0
    )
    back_rows = jnp.concatenate([back_rows_a, lay_cols(pieces_b, place, size)], axis=0)
    grad_mixed = contract_features(back_rows, out_all)
    x_down, y_down = send_chips(held_down, rows)
    out_part = contract_tokens(mixed, back_rows).astype(BF)
    out_part, mlp_grad, grad_mixed, result_cut = fence(out_part, mlp_grad, grad_mixed, result_cut)
    out_grad = lax.psum_scatter(out_part, "row", scatter_dimension=1, tiled=True)
    result_a = send_cols([piece[first] for piece in result_cut[1]], size)
    lows = mixer_backward(heads, dk, dv, pres, shared, grad_mixed, saved)
    lows, x_down, y_down, result_a = fence(lows, x_down, y_down, result_a)
    *lows, low_small, query_taps, key_taps, value_taps, params_part, gain_part = lows
    low = jnp.concatenate(lows + [low_small], axis=1)
    down_late = last_step(held_down, x_down, y_down, rows)

    in_part = contract_tokens(hidden, low).astype(BF)
    in_grad = lax.psum_scatter(in_part, "row", scatter_dimension=0, tiled=True)
    hidden_part = contract_features(after(low, in_part), in_all)
    inner = jnp.sum(hidden_part * first_gains * wide_all, axis=1)
    hidden_cut = cut_cols(hidden_part, place, size)
    first_gain_part = jnp.sum(hidden_part * wide_all * first_scale, axis=0)
    notes = [
        jnp.concatenate(
            [inner, lax.dynamic_slice(first_gain_part, ((place ^ step) * width,), (width,)), gain_part[0]]
        )
        for step in range(size)
    ]
    notes, hidden_cut, down_late, result_later = fence(notes, hidden_cut, down_late, result_cut[1])

    noted = sum([notes[0]] + send_cols(notes[1:], size))
    hidden_got = send_cols(hidden_cut[1], size)
    result_b = send_cols([piece[last] for piece in result_later], size)
    first_inner, gains = noted[:tokens, None], noted[tokens:]
    sums = [query_taps, key_taps, value_taps, params_part[0:2, :heads], second_gain_part, gains]
    query_taps, key_taps, value_taps, params_grad, second_gain_grad, gains = lax.psum(sums, "row")
    norm_gain_grad, gain_grad = gains[:width], gains[width:]
    result = residual + result_cut[0]
    result = jnp.concatenate([add_cols(result[first], result_a), add_cols(result[last], result_b)], axis=0)
    down_grad = finish(*down_late).T
    mlp_grad = mlp_grad.astype(F32)
    out_grad = out_grad.astype(F32)
    hidden_got, noted, down_grad, mlp_grad, out_grad, query_taps, result = fence(
        hidden_got, noted, down_grad, mlp_grad, out_grad, query_taps, result
    )

    grad_hidden = add_cols(hidden_cut[0], hidden_got)
    grad_inputs = (
        grad_residual
        + first_scale * norm_gain * grad_hidden
        - wide_inputs * (first_scale * first_scale * first_scale * first_inner / model)
    )
    in_grad, result, grad_inputs = fence(in_grad, result, grad_inputs)

    def head_columns(start, stop):
        return in_grad[:, heads * start : heads * stop].astype(F32)

    return (
        result,
        grad_inputs,
        norm_gain_grad,
        head_columns(0, dk),
        head_columns(dk, 2 * dk),
        head_columns(2 * dk, 2 * dk + dv),
        head_columns(2 * dk + dv, wide),
        in_grad[:, heads * wide : heads * wide + heads].astype(F32),
        in_grad[:, heads * wide + heads : heads * wide + 2 * heads].astype(F32),
        query_taps,
        key_taps,
        value_taps,
        params_grad[0],
        params_grad[1],
        gain_grad,
        out_grad,
        second_gain_grad,
        mlp_grad[:, :hidden_units],
        mlp_grad[:, hidden_units:],
        down_grad,
    )


ROW_COL = P("row", "col")
COL_ROW = P("col", "row")
PLACED = (
    ROW_COL, P("row"), P("col"),
    ROW_COL, ROW_COL, ROW_COL, ROW_COL, ROW_COL, ROW_COL,
    P(None, "col"), P(None, "col"), P(None, "col"),
    P("col"), P("col"), P(),
    COL_ROW, P("col"), ROW_COL, ROW_COL, COL_ROW, ROW_COL,
)
MADE = (
    ROW_COL, ROW_COL, P("col"),
    ROW_COL, ROW_COL, ROW_COL, ROW_COL, ROW_COL, ROW_COL,
    P(None, "col"), P(None, "col"), P(None, "col"),
    P("col"), P("col"), P(),
    COL_ROW, P("col"), ROW_COL, ROW_COL, COL_ROW,
)


def solution(mesh):
    return jax.shard_map(per_device, mesh=mesh, in_specs=PLACED, out_specs=MADE, check_vma=False)
```
